256 devices in a mesh: azim: 64 (over x, y_hi, z), axial: 4 (over y_lo, core).
Axes of the slice: x: 4, y: 4 (y_hi: 2, y_lo: 2; y = y_hi * 2 + y_lo), z: 8, core: 2. Of those that a mesh axis runs over, the one named last changes fastest.
Arguments:
- rhs: float32 [64, 48, 4, 128], P('azim', None, 'axial'), may hold values from -6 to 6
- coupling: float32 [64, 48, 4, 128], P('azim', None, 'axial'), may hold values from 0.2 to 0.5
- fwd_coupling: bfloat16 [64, 48, 48, 4, 128], P('azim', None, None, 'axial'), may hold values from -1 to 1
- bwd_coupling: bfloat16 [64, 48, 48, 4, 128], P('azim', None, None, 'axial'), may hold values from -1 to 1
- block_inverse: bfloat16 [64, 48, 48, 4, 128], P('azim', None, None, 'axial'), may hold values from -1 to 1
Outputs:
- correction: float32 [64, 48, 4, 128], P('azim', None, 'axial')
- remaining: float32 [64, 48, 4, 128], P('azim', None, 'axial')
The draws below stay inside these ranges and needn't reach their ends.
All inputs are finite; a program needn't handle non-finite values.
Results may differ from the reference program's by a relative error of at most 0.0003.
Values sent between devices are 32-bit elements; how exact they have to be, the bound alone decides.
A program may use at most 128 MiB of HBM per device.

```python
import math
import jax
import jax.numpy as jnp
from jax import lax

B = 48
GAP_LAYERS = 128
ANGULAR_PANELS = 64
FLOW_POSITIONS = 4


def coupling_blocks(key, slow_share, orient):
    divided_seeds = jax.random.split(key, 8)
    half = B // 2
    picker = jax.random.uniform(divided_seeds[0], (1, half, FLOW_POSITIONS, GAP_LAYERS))
    speed = jax.random.uniform(divided_seeds[1], (1, half, FLOW_POSITIONS, GAP_LAYERS), minval=0.4, maxval=1.0)
    factor = jnp.exp(jax.random.uniform(divided_seeds[2], (ANGULAR_PANELS, half, FLOW_POSITIONS, GAP_LAYERS), minval=math.log(0.5), maxval=math.log(2.0)))
    slow_rate = jnp.minimum(jnp.exp(-speed * factor / ANGULAR_PANELS), 0.998)
    fast_rate = jax.random.uniform(divided_seeds[3], (ANGULAR_PANELS, half, FLOW_POSITIONS, GAP_LAYERS), minval=0.3, maxval=0.8)
    coupled_speed = jnp.where(picker < slow_share, slow_rate, fast_rate)
    packet_bundles = jax.random.uniform(divided_seeds[4], (ANGULAR_PANELS, 1, FLOW_POSITIONS, GAP_LAYERS)) < 2.0 / ANGULAR_PANELS
    coupled_speed = coupled_speed * jnp.where(packet_bundles, 0.75, 1.0)
    turning = jax.random.uniform(divided_seeds[5], (ANGULAR_PANELS, half, FLOW_POSITIONS, GAP_LAYERS), minval=0.3, maxval=0.8)
    turning = turning * jnp.where(jax.random.uniform(divided_seeds[6], (ANGULAR_PANELS, half, FLOW_POSITIONS, GAP_LAYERS)) < 0.5, 1.0, -1.0)
    rate_rows = jnp.repeat(coupled_speed, 2, axis=1)[:, :, None]
    cosine = jnp.repeat(jnp.cos(turning), 2, axis=1)[:, :, None]
    sine = jnp.repeat(jnp.sin(turning), 2, axis=1)[:, :, None]
    row_index = lax.broadcasted_iota(jnp.int32, (1, B, B, 1, 1), 1)
    column_index = lax.broadcasted_iota(jnp.int32, (1, B, B, 1, 1), 2)
    same_pair = row_index // 2 == column_index // 2
    on_diagonal = row_index == column_index
    upper_row = row_index % 2 == 0
    paired = jnp.where(on_diagonal, cosine, jnp.where(upper_row, -sine, sine)) * rate_rows
    structured = jnp.where(same_pair, paired, 0.0) * orient
    noise = jnp.clip(jax.random.normal(divided_seeds[7], (ANGULAR_PANELS, B, B, FLOW_POSITIONS, GAP_LAYERS)), -4.0, 4.0) * (0.02 / math.sqrt(B))
    return (structured + noise).astype(jnp.bfloat16)


def draw_fwd_coupling(key, part):
    share = 0.5
    return coupling_blocks(jax.random.fold_in(key, 11), share, 1.0)


def draw_bwd_coupling(key, part):
    share = 0.5
    return coupling_blocks(jax.random.fold_in(key, 12), share, -1.0)


def draw_block_inverse(key, part):
    divided_seeds = jax.random.split(jax.random.fold_in(key, 13), 2)
    diagonal = jnp.exp(jax.random.uniform(divided_seeds[0], (ANGULAR_PANELS, B, 1, FLOW_POSITIONS, GAP_LAYERS), minval=math.log(0.04), maxval=math.log(0.15)))
    noise = jnp.clip(jax.random.normal(divided_seeds[1], (ANGULAR_PANELS, B, B, FLOW_POSITIONS, GAP_LAYERS)), -4.0, 4.0) * (0.07 / math.sqrt(B))
    row_index = lax.broadcasted_iota(jnp.int32, (1, B, B, 1, 1), 1)
    column_index = lax.broadcasted_iota(jnp.int32, (1, B, B, 1, 1), 2)
    return jnp.where(row_index == column_index, diagonal, noise).astype(jnp.bfloat16)


def block_levels(own_key, extent, shards, low, top_value):
    factor_of = 1.0
    for axis_at, blocks in shards:
        heights = jax.random.uniform(jax.random.fold_in(jax.random.fold_in(own_key, 6), axis_at), (blocks,), jnp.float32, low / len(shards), top_value / len(shards))
        factor_of = factor_of * jnp.repeat(jnp.exp(heights), extent[axis_at] // blocks).reshape((-1,) + (1,) * (len(extent) - 1 - axis_at))
    return factor_of


def bell_draw(own_key, extent, scale, bound, pieces=(), held_as=jnp.bfloat16):
    level = block_levels(own_key, extent, pieces, -0.22, 0.18) if pieces else 1.0
    entries = jax.random.normal(own_key, extent, jnp.float32) * scale * level
    return jnp.minimum(jnp.maximum(entries, -bound), bound).astype(held_as)


def setup_inputs(seed: int = 0) -> dict:
    seeds = jax.random.split(jax.random.key(seed), 6)
    rhs = bell_draw(seeds[0], (ANGULAR_PANELS, B, FLOW_POSITIONS, GAP_LAYERS), 1.0, 6.0, ((0, 64), (2, 4)), jnp.float32)
    coupling = jnp.clip(0.2 + 0.3 * jax.random.uniform(seeds[1], (ANGULAR_PANELS, B, FLOW_POSITIONS, GAP_LAYERS), jnp.float32) ** block_levels(seeds[1], (ANGULAR_PANELS, B, FLOW_POSITIONS, GAP_LAYERS), ((0, 64), (2, 4)), -0.2, 0.2), 0.2, 0.5)
    fwd_coupling = draw_fwd_coupling(jax.random.fold_in(seeds[5], 71), 0)
    bwd_coupling = draw_bwd_coupling(jax.random.fold_in(seeds[5], 71), 0)
    block_inverse = draw_block_inverse(jax.random.fold_in(seeds[5], 71), 0)
    return dict(rhs=rhs, coupling=coupling, fwd_coupling=fwd_coupling, bwd_coupling=bwd_coupling, block_inverse=block_inverse)


def reference(rhs, coupling, fwd_coupling, bwd_coupling, block_inverse):
    line_count = FLOW_POSITIONS * GAP_LAYERS
    forward_blocks = fwd_coupling.reshape(ANGULAR_PANELS, B, B, line_count)
    backward_blocks = bwd_coupling.reshape(ANGULAR_PANELS, B, B, line_count)
    inverse_blocks = block_inverse.reshape(ANGULAR_PANELS, B, B, line_count)
    source = rhs.reshape(ANGULAR_PANELS, B, line_count)
    coupling_field = coupling.reshape(ANGULAR_PANELS, B, line_count)

    def sweep(blocks, consts, reverse):
        def advance(carried, inputs):
            one_block, const_term = inputs
            carried = const_term - jnp.einsum("abl,al->bl", one_block.astype(jnp.float32), carried,
                                              precision=lax.Precision.HIGHEST)
            return carried, carried

        start_state = jnp.zeros((B, line_count), jnp.float32)
        wrapped, _ = lax.scan(advance, start_state, (blocks, consts), reverse=reverse)
        _, outputs = lax.scan(advance, wrapped, (blocks, consts), reverse=reverse)
        return outputs

    def precondition(vector):
        consts = lax.map(lambda members: jnp.einsum("abl,al->bl", members[0].astype(jnp.float32), members[1],
                                                    precision=lax.Precision.HIGHEST), (inverse_blocks, vector))
        forward = sweep(forward_blocks, consts, False)
        return sweep(backward_blocks, forward, True)

    def neighbours(field):
        grid = field.reshape(ANGULAR_PANELS, B, FLOW_POSITIONS, GAP_LAYERS)
        padded = jnp.pad(grid, ((0, 0), (0, 0), (1, 1), (0, 0)))
        return (padded[:, :, :-2] + padded[:, :, 2:]).reshape(ANGULAR_PANELS, B, line_count)

    applied_once = precondition(source)
    middle = source - applied_once + coupling_field * neighbours(applied_once)
    second = precondition(middle)
    correction = applied_once + second
    remaining = middle - second + coupling_field * neighbours(second)
    return correction.reshape(ANGULAR_PANELS, B, FLOW_POSITIONS, GAP_LAYERS), remaining.reshape(ANGULAR_PANELS, B, FLOW_POSITIONS, GAP_LAYERS)
```

```python
import functools

import jax
import jax.numpy as jnp
from jax import lax
from jax.experimental import pallas as pl
from jax.experimental.pallas import tpu as pltpu
from jax.sharding import PartitionSpec as P

MESH = pl.DeviceIdType.MESH
W = 48
L = 128
RUN = 8
PIECES = W * W // L
ROWS = PIECES * 16
CHUNKS = 2
CROWS = ROWS // CHUNKS
CPIECES = PIECES // CHUNKS
FWD, BWD, INV = 0, 1, 2


def aligned(start, size):
    return pl.ds(pl.multiple_of(start, 8), size)


def wait_bytes(ref, sem):
    pltpu.make_async_copy(ref, ref, sem).wait()


def matvec(load, vec_ref):
    def body(step, acc):
        for inner in range(8):
            a = step * 8 + inner
            block = load(a).reshape(6, 8, L)
            acc = acc + block * vec_ref[pl.ds(a, 8, stride=0), :][None]
        return acc

    acc = lax.fori_loop(0, W // 8, body, jnp.zeros((6, 8, L), jnp.float32))
    return acc.reshape(W, L)


def kernel(
    rhs, coup, fwd, bwd, inv, corr, rem,
    s1, r1, s2, r2, maps, early, inv_t,
    vec, stage, v1, w1, v2, w2, o1, p1, o2, p2, halo_out, halo_in,
    c_t, rhs_t, coup_t, first, middle,
    mz_send, mz_recv, mg_send, mg_recv, v_send, v_recv, h_send, h_recv,
):
    me = lax.axis_index("azim")
    station = lax.axis_index("axial")
    z = lax.rem(me, RUN)
    g = me // RUN
    blocks = (fwd, bwd, inv)

    def z_peer(i):
        return {"azim": g * RUN + lax.rem(z + i, RUN)}

    def g_peer(i):
        return {"azim": lax.rem(g + i, RUN) * RUN + z}

    up = {"axial": lax.rem(station + 1, 4)}
    down = {"axial": lax.rem(station + 3, 4)}

    lane = lax.broadcasted_iota(jnp.int32, (W, L), 1)
    lane_z = lax.rem(lane, RUN)
    lane_g = lane // 16

    barrier = pltpu.get_barrier_semaphore()

    def greet(i, _):
        pl.semaphore_signal(barrier, inc=1, device_id=z_peer(i), device_id_type=MESH)
        pl.semaphore_signal(barrier, inc=1, device_id=g_peer(i), device_id_type=MESH)
        return 0

    lax.fori_loop(1, RUN, greet, 0)
    pl.semaphore_signal(barrier, inc=1, device_id=up, device_id_type=MESH)
    pl.semaphore_signal(barrier, inc=1, device_id=down, device_id_type=MESH)

    def remote(src, dst, send, recv, device):
        pltpu.make_async_remote_copy(
            src_ref=src, dst_ref=dst, send_sem=send, recv_sem=recv,
            device_id=device, device_id_type=MESH,
        ).start()

    def pack(kind):
        def body(t, _):
            piece = blocks[kind][pl.ds(pl.multiple_of(t * L, L), L), :].astype(jnp.float32).T
            for zo in range(RUN):
                s1[kind, aligned(zo * ROWS + t * 16, 16)] = piece[zo * 16 : zo * 16 + 16]
            return 0

        lax.fori_loop(0, PIECES, body, 0)

    def send_z(kind):
        for chunk in range(CHUNKS):

            def body(i, _, chunk=chunk):
                to = lax.rem(z + i, RUN)
                remote(
                    s1.at[kind, aligned(to * ROWS + chunk * CROWS, CROWS)],
                    r1.at[kind, aligned(z * ROWS + chunk * CROWS, CROWS)],
                    mz_send.at[kind, chunk], mz_recv.at[kind, chunk], z_peer(i),
                )
                return 0

            lax.fori_loop(1, RUN, body, 0)
        r1[kind, aligned(z * ROWS, ROWS)] = s1[kind, aligned(z * ROWS, ROWS)]

    def forward_g(kind):
        for chunk in range(CHUNKS):
            wait_bytes(r1.at[kind, pl.ds(0, 7 * CROWS)], mz_recv.at[kind, chunk])

            def body(t, _):
                for q in range(16):
                    s2[kind, aligned((q // 2) * ROWS + t * 16 + (q % 2) * 8, 8)] = r1[
                        kind, pl.ds(t * 16 + q, 8, stride=ROWS), :
                    ]
                return 0

            lax.fori_loop(chunk * CPIECES, (chunk + 1) * CPIECES, body, 0)

            def send(i, _, chunk=chunk):
                to = lax.rem(g + i, RUN)
                remote(
                    s2.at[kind, aligned(to * ROWS + chunk * CROWS, CROWS)],
                    r2.at[kind, aligned(g * ROWS + chunk * CROWS, CROWS)],
                    mg_send.at[kind, chunk], mg_recv.at[kind, chunk], g_peer(i),
                )
                return 0

            lax.fori_loop(1, RUN, send, 0)
        r2[kind, aligned(g * ROWS, ROWS)] = s2[kind, aligned(g * ROWS, ROWS)]

    def unpack(kind):
        for chunk in range(CHUNKS):
            wait_bytes(r2.at[kind, pl.ds(0, 7 * CROWS)], mg_recv.at[kind, chunk])

            def body(t, _):
                rows = [r2[kind, aligned(run * ROWS + t * 16, 16)] for run in range(RUN)]
                piece = jnp.concatenate(rows, axis=0).T
                if kind == INV:
                    inv_t[pl.ds(pl.multiple_of(t * L, L), L), :] = piece
                else:
                    maps[kind, 0, pl.ds(pl.multiple_of(t * L, L), L), :] = -piece
                return 0

            lax.fori_loop(chunk * CPIECES, (chunk + 1) * CPIECES, body, 0)

    def earlier(value, distance, kind):
        return pltpu.roll(value, distance if kind == FWD else L - distance, 1)

    def inside(distance, kind):
        return lane_z >= distance if kind == FWD else lane_z < RUN - distance

    def compose(kind, level):
        distance = 1 << level
        exists = inside(distance, kind)
        sub = lax.broadcasted_iota(jnp.int32, (W, L), 0)

        def shift(a, _):
            moved = earlier(maps[kind, level, aligned(a * W, W)], distance, kind)
            early[aligned(a * W, W)] = jnp.where(exists, moved, jnp.where(sub == a, 1.0, 0.0))
            return 0

        lax.fori_loop(0, W, shift, 0)

        def product(four, _):
            def over(step, acc):
                acc = list(acc)
                for inner in range(8):
                    c = step * 8 + inner
                    later = maps[kind, level, aligned(c * W, W)].reshape(6, 8, L)
                    for i in range(4):
                        factor = early[pl.ds((four * 4 + i) * W + c, 8, stride=0), :]
                        acc[i] = acc[i] + later * factor[None]
                return tuple(acc)

            zero = jnp.zeros((6, 8, L), jnp.float32)
            acc = lax.fori_loop(0, W // 8, over, (zero,) * 4)
            for i in range(4):
                maps[kind, level + 1, aligned((four * 4 + i) * W, W)] = acc[i].reshape(W, L)
            return 0

        lax.fori_loop(0, W // 4, product, 0)

    def apply_map(kind, level):
        return matvec(lambda a: maps[kind, level, aligned(a * W, W)], vec)

    def sweep(kind, value):
        state = value
        for level in range(3):
            distance = 1 << level
            moved = earlier(state, distance, kind)
            vec[0:W] = jnp.where(inside(distance, kind), moved, 0.0)
            state = state + apply_map(kind, level)
        order = lane_g if kind == FWD else RUN - 1 - lane_g

        def run_step(n, carry):
            running, entering = carry
            moved = earlier(running, 16, kind)
            entering = jnp.where(order == n - RUN, moved, entering)
            vec[0:W] = moved
            return state + apply_map(kind, 3), entering

        running, entering = lax.fori_loop(1, 15, run_step, (state, jnp.zeros((W, L), jnp.float32)))
        entering = jnp.where(order == RUN - 1, earlier(running, 16, kind), entering)
        place = RUN - 1 - lane_z if kind == FWD else lane_z
        for distance in (1, 2, 4):
            back = pltpu.roll(entering, L - distance if kind == FWD else distance, 1)
            entering = jnp.where(place < distance, entering, back)
        vec[0:W] = entering
        return state + apply_map(kind, 3)

    stage[...] = jnp.zeros((2, L, L), jnp.float32)
    vec[0:W] = rhs[...]
    stage[0, 0:W] = matvec(lambda a: inv[pl.ds(pl.multiple_of(a * W, 16), W), :].astype(jnp.float32), vec)
    stage[0, W : 2 * W] = rhs[...]
    stage[1, 0:W] = coup[...]
    for block in range(2):
        turned = stage[block].T
        for zo in range(RUN):
            v1[pl.ds(zo * 32 + block * 16, 16)] = turned[zo * 16 : zo * 16 + 16]
    pack(FWD)
    pl.semaphore_wait(barrier, 16)

    def send_v1(i, _):
        to = lax.rem(z + i, RUN)
        remote(v1.at[aligned(to * 32, 32)], w1.at[aligned(z * 32, 32)], v_send.at[0], v_recv.at[0], z_peer(i))
        return 0

    lax.fori_loop(1, RUN, send_v1, 0)
    w1[aligned(z * 32, 32)] = v1[aligned(z * 32, 32)]
    send_z(FWD)
    pack(BWD)
    pack(INV)
    wait_bytes(w1.at[pl.ds(0, 7 * 32)], v_recv.at[0])
    for block in range(2):
        for q in range(16):
            v2[pl.ds((q // 2) * 32 + block * 16 + (q % 2) * 8, 8)] = w1[pl.ds(block * 16 + q, 8, stride=32), :]

    def send_v2(i, _):
        to = lax.rem(g + i, RUN)
        remote(v2.at[aligned(to * 32, 32)], w2.at[aligned(g * 32, 32)], v_send.at[1], v_recv.at[1], g_peer(i))
        return 0

    lax.fori_loop(1, RUN, send_v2, 0)
    w2[aligned(g * 32, 32)] = v2[aligned(g * 32, 32)]
    forward_g(FWD)
    send_z(BWD)
    wait_bytes(w2.at[pl.ds(0, 7 * 32)], v_recv.at[1])
    turned = [
        jnp.concatenate([w2[pl.ds(run * 32 + block * 16, 16)] for run in range(RUN)], axis=0).T for block in range(2)
    ]
    c_t[...] = turned[0][0:W]
    rhs_t[...] = turned[0][W : 2 * W]
    coup_t[...] = turned[1][0:W]

    unpack(FWD)
    compose(FWD, 0)
    compose(FWD, 1)
    forward_g(BWD)
    send_z(INV)
    compose(FWD, 2)
    halfway = sweep(FWD, c_t[...])
    c_t[...] = halfway
    unpack(BWD)
    compose(BWD, 0)
    compose(BWD, 1)
    compose(BWD, 2)
    forward_g(INV)

    def stations_sum(turn, value):
        halo_out[turn] = value
        remote(halo_out.at[turn], halo_in.at[turn, 0], h_send.at[turn, 0], h_recv.at[turn, 0], up)
        remote(halo_out.at[turn], halo_in.at[turn, 1], h_send.at[turn, 1], h_recv.at[turn, 1], down)
        for side in range(2):
            wait_bytes(halo_in.at[turn, side], h_recv.at[turn, side])
            wait_bytes(halo_out.at[turn], h_send.at[turn, side])
        below = jnp.where(station > 0, halo_in[turn, 0], 0.0)
        above = jnp.where(station < 3, halo_in[turn, 1], 0.0)
        return below + above

    first[...] = sweep(BWD, c_t[...])
    middle[...] = rhs_t[...] - first[...] + coup_t[...] * stations_sum(0, first[...])
    unpack(INV)
    vec[0:W] = middle[...]
    c_t[...] = sweep(FWD, matvec(lambda a: inv_t[aligned(a * W, W)], vec))
    second = sweep(BWD, c_t[...])
    c_t[...] = second
    stage[0, 0:W] = first[...] + second
    stage[0, W : 2 * W] = middle[...] - c_t[...] + coup_t[...] * stations_sum(1, c_t[...])

    o1[...] = stage[0].T

    def send_o1(i, _):
        to = lax.rem(g + i, RUN)
        remote(o1.at[aligned(to * 16, 16)], p1.at[aligned(g * 16, 16)], v_send.at[2], v_recv.at[2], g_peer(i))
        return 0

    lax.fori_loop(1, RUN, send_o1, 0)
    p1[aligned(g * 16, 16)] = o1[aligned(g * 16, 16)]
    wait_bytes(p1.at[pl.ds(0, 7 * 16)], v_recv.at[2])
    for q in range(16):
        o2[pl.ds(q, 8, stride=16), :] = p1[pl.ds(q * 8, 8)]

    def send_o2(i, _):
        to = lax.rem(z + i, RUN)
        remote(o2.at[aligned(to * 16, 16)], p2.at[aligned(z * 16, 16)], v_send.at[3], v_recv.at[3], z_peer(i))
        return 0

    lax.fori_loop(1, RUN, send_o2, 0)
    p2[aligned(z * 16, 16)] = o2[aligned(z * 16, 16)]
    wait_bytes(p2.at[pl.ds(0, 7 * 16)], v_recv.at[3])
    final = p2[...].T
    corr[...] = final[0:W]
    rem[...] = final[W : 2 * W]

    for kind in range(3):
        for chunk in range(CHUNKS):
            wait_bytes(s1.at[kind, pl.ds(0, 7 * CROWS)], mz_send.at[kind, chunk])
            wait_bytes(s2.at[kind, pl.ds(0, 7 * CROWS)], mg_send.at[kind, chunk])
    for at, ref in ((0, v1), (1, v2)):
        wait_bytes(ref.at[pl.ds(0, 7 * 32)], v_send.at[at])
    for at, ref in ((2, o1), (3, o2)):
        wait_bytes(ref.at[pl.ds(0, 7 * 16)], v_send.at[at])


def on_device(rhs, coupling, fwd_coupling, bwd_coupling, block_inverse):
    f32 = jnp.float32
    vmem = pl.BlockSpec(memory_space=pltpu.VMEM)
    dma = pltpu.SemaphoreType.DMA
    mat = pltpu.VMEM((3, W * W, L), f32)
    small = pltpu.VMEM((W, L), f32)
    square = pltpu.VMEM((L, L), f32)
    wide = pltpu.VMEM((2 * L, L), f32)
    corr, rem = pl.pallas_call(
        kernel,
        out_shape=(jax.ShapeDtypeStruct((W, L), f32),) * 2,
        in_specs=[vmem] * 5,
        out_specs=(vmem, vmem),
        scratch_shapes=[
            mat, pltpu.VMEM((3, W * W + ROWS, L), f32), mat, mat,
            pltpu.VMEM((2, 4, W * W, L), f32), pltpu.VMEM((W * W + 8, L), f32), pltpu.VMEM((W * W, L), f32),
            pltpu.VMEM((W + 8, L), f32), pltpu.VMEM((2, L, L), f32),
            wide, pltpu.VMEM((2 * L + 32, L), f32), wide, wide, square, square, pltpu.VMEM((L + 16, L), f32), square,
            pltpu.VMEM((2, W, L), f32), pltpu.VMEM((2, 2, W, L), f32),
            small, small, small, small, small,
            dma((3, CHUNKS)), dma((3, CHUNKS)), dma((3, CHUNKS)), dma((3, CHUNKS)),
            dma((4,)), dma((4,)), dma((2, 2)), dma((2, 2)),
        ],
        compiler_params=pltpu.CompilerParams(
            collective_id=0, has_side_effects=True, vmem_limit_bytes=48 << 20
        ),
        name="both_applies",
    )(
        rhs.reshape(W, L), coupling.reshape(W, L), fwd_coupling.reshape(W * W, L),
        bwd_coupling.reshape(W * W, L), block_inverse.reshape(W * W, L),
    )
    return corr.reshape(rhs.shape), rem.reshape(rhs.shape)


def solution(mesh):
    vector = P("azim", None, "axial", None)
    matrix = P("azim", None, None, "axial", None)
    return jax.shard_map(
        on_device,
        mesh=mesh,
        in_specs=(vector, vector, matrix, matrix, matrix),
        out_specs=(vector, vector),
        check_vma=False,
    )
```

```python
import functools

import jax
import jax.numpy as jnp
from jax import lax
from jax.experimental import pallas as pl
from jax.experimental.pallas import tpu as pltpu
from jax.sharding import PartitionSpec as P

MESH = pl.DeviceIdType.MESH
W = 48
L = 128
RUN = 8
PIECES = W * W // L
ROWS = PIECES * 16
CHUNKS = 3
EAGER = 2
CROWS = ROWS // CHUNKS
CPIECES = PIECES // CHUNKS
FWD, BWD, INV = 0, 1, 2


def aligned(start, size):
    return pl.ds(start if isinstance(start, int) else pl.multiple_of(start, 8), size)


def wait_bytes(ref, sem):
    pltpu.make_async_copy(ref, ref, sem).wait()


def matvec(load, vec_ref):
    acc = jnp.zeros((6, 8, L), jnp.float32)
    for a in range(W):
        acc = acc + load(a).reshape(6, 8, L) * vec_ref[pl.ds(a, 8, stride=0), :][None]
    return acc.reshape(W, L)


def kernel(
    rhs_in, coup_in, fwd_in, bwd_in, inv_in, corr, rem, rhs, coup, blocks, in_sem,
    s1, r1, s2, r2, maps, early, inv_t,
    vec, stage, v1, w1, v2, w2, o1, p1, o2, p2, halo_out, halo_in,
    c_t, rhs_t, coup_t, first, middle,
    mz_send, mz_recv, mg_send, mg_recv, v_send, v_recv, h_send, h_recv,
):
    me = lax.axis_index("azim")
    station = lax.axis_index("axial")
    z = lax.rem(me, RUN)
    g = me // RUN
    loads = [
        pltpu.make_async_copy(src, dst, in_sem.at[at])
        for at, (src, dst) in enumerate((
            (fwd_in, blocks.at[FWD]), (rhs_in, rhs), (coup_in, coup), (inv_in, blocks.at[INV]), (bwd_in, blocks.at[BWD]),
        ))
    ]
    for load in loads:
        load.start()

    def z_peer(i):
        return {"azim": g * RUN + lax.rem(z + i, RUN)}

    def g_peer(i):
        return {"azim": lax.rem(g + i, RUN) * RUN + z}

    up = {"axial": lax.rem(station + 1, 4)}
    down = {"axial": lax.rem(station + 3, 4)}

    lane = lax.broadcasted_iota(jnp.int32, (W, L), 1)
    lane_z = lax.rem(lane, RUN)
    lane_g = lane // 16

    barrier = pltpu.get_barrier_semaphore()

    def greet(i, _):
        pl.semaphore_signal(barrier, inc=1, device_id=z_peer(i), device_id_type=MESH)
        pl.semaphore_signal(barrier, inc=1, device_id=g_peer(i), device_id_type=MESH)
        return 0

    lax.fori_loop(1, RUN, greet, 0)
    pl.semaphore_signal(barrier, inc=1, device_id=up, device_id_type=MESH)
    pl.semaphore_signal(barrier, inc=1, device_id=down, device_id_type=MESH)

    def remote(src, dst, send, recv, device):
        pltpu.make_async_remote_copy(
            src_ref=src, dst_ref=dst, send_sem=send, recv_sem=recv,
            device_id=device, device_id_type=MESH,
        ).start()

    def pack(kind, chunk):
        def body(step, _):
            for inner in range(3):
                t = step * 3 + inner
                piece = blocks[kind, pl.ds(pl.multiple_of(t * L, L), L), :].astype(jnp.float32).T
                for zo in range(RUN):
                    s1[kind, aligned(zo * ROWS + t * 16, 16)] = piece[zo * 16 : zo * 16 + 16]
            return 0

        lax.fori_loop(chunk * CPIECES // 3, (chunk + 1) * CPIECES // 3, body, 0)

    def send_z(kind, chunk):
        for i in range(1, RUN):
            to = lax.rem(z + i, RUN)
            remote(
                s1.at[kind, aligned(to * ROWS + chunk * CROWS, CROWS)],
                r1.at[kind, aligned(z * ROWS + chunk * CROWS, CROWS)],
                mz_send.at[kind, chunk], mz_recv.at[kind, chunk], z_peer(i),
            )
        own = aligned(z * ROWS + chunk * CROWS, CROWS)
        r1[kind, own] = s1[kind, own]

    def forward_g(kind, chunk):
        wait_bytes(r1.at[kind, pl.ds(0, 7 * CROWS)], mz_recv.at[kind, chunk])

        def body(t, _):
            for q in range(16):
                s2[kind, aligned((q // 2) * ROWS + t * 16 + (q % 2) * 8, 8)] = r1[
                    kind, pl.ds(t * 16 + q, 8, stride=ROWS), :
                ]
            return 0

        lax.fori_loop(chunk * CPIECES, (chunk + 1) * CPIECES, body, 0)
        for i in range(1, RUN):
            to = lax.rem(g + i, RUN)
            remote(
                s2.at[kind, aligned(to * ROWS + chunk * CROWS, CROWS)],
                r2.at[kind, aligned(g * ROWS + chunk * CROWS, CROWS)],
                mg_send.at[kind, chunk], mg_recv.at[kind, chunk], g_peer(i),
            )
        own = aligned(g * ROWS + chunk * CROWS, CROWS)
        r2[kind, own] = s2[kind, own]

    def unpack(kind, chunk):
        wait_bytes(r2.at[kind, pl.ds(0, 7 * CROWS)], mg_recv.at[kind, chunk])

        def body(step, _):
            for inner in range(3):
                t = step * 3 + inner
                rows = [r2[kind, aligned(run * ROWS + t * 16, 16)] for run in range(RUN)]
                piece = jnp.concatenate(rows, axis=0).T
                if kind == INV:
                    inv_t[pl.ds(pl.multiple_of(t * L, L), L), :] = piece
                else:
                    maps[kind, 0, pl.ds(pl.multiple_of(t * L, L), L), :] = -piece
            return 0

        lax.fori_loop(chunk * CPIECES // 3, (chunk + 1) * CPIECES // 3, body, 0)

    def earlier(value, distance, kind):
        return pltpu.roll(value, distance if kind == FWD else L - distance, 1)

    def inside(distance, kind):
        return lane_z >= distance if kind == FWD else lane_z < RUN - distance

    def compose(kind, level):
        distance = 1 << level
        exists = inside(distance, kind)
        sub = lax.broadcasted_iota(jnp.int32, (W, L), 0)

        def shift(step, _):
            for inner in range(8):
                a = step * 8 + inner
                moved = earlier(maps[kind, level, aligned(a * W, W)], distance, kind)
                early[aligned(a * W, W)] = jnp.where(exists, moved, jnp.where(sub == a, 1.0, 0.0))
            return 0

        lax.fori_loop(0, W // 8, shift, 0)

        def product(four, _):
            acc = [jnp.zeros((6, 8, L), jnp.float32)] * 4
            for c in range(W):
                later = maps[kind, level, pl.ds(c * W, W)].reshape(6, 8, L)
                for i in range(4):
                    factor = early[pl.ds((four * 4 + i) * W + c, 8, stride=0), :]
                    acc[i] = acc[i] + later * factor[None]
            for i in range(4):
                maps[kind, level + 1, aligned((four * 4 + i) * W, W)] = acc[i].reshape(W, L)
            return 0

        lax.fori_loop(0, W // 4, product, 0)

    def apply_map(kind, level):
        return matvec(lambda a: maps[kind, level, pl.ds(a * W, W)], vec)

    def sweep(kind, value):
        state = value
        for level in range(3):
            distance = 1 << level
            moved = earlier(state, distance, kind)
            vec[0:W] = jnp.where(inside(distance, kind), moved, 0.0)
            state = state + apply_map(kind, level)
        order = lane_g if kind == FWD else RUN - 1 - lane_g

        def run_step(n, carry):
            running, entering = carry
            moved = earlier(running, 16, kind)
            entering = jnp.where(order == n - RUN, moved, entering)
            vec[0:W] = moved
            return state + apply_map(kind, 3), entering

        running, entering = lax.fori_loop(1, 15, run_step, (state, jnp.zeros((W, L), jnp.float32)))
        entering = jnp.where(order == RUN - 1, earlier(running, 16, kind), entering)
        place = RUN - 1 - lane_z if kind == FWD else lane_z
        for distance in (1, 2, 4):
            back = pltpu.roll(entering, L - distance if kind == FWD else distance, 1)
            entering = jnp.where(place < distance, entering, back)
        vec[0:W] = entering
        return state + apply_map(kind, 3)

    def send_vectors():
        stage[...] = jnp.zeros((2, L, L), jnp.float32)
        for load in loads[1:4]:
            load.wait()
        vec[0:W] = rhs[...]
        stage[0, 0:W] = matvec(lambda a: blocks[INV, pl.ds(a * W, W), :].astype(jnp.float32), vec)
        stage[0, W : 2 * W] = rhs[...]
        stage[1, 0:W] = coup[...]
        for block in range(2):
            turned = stage[block].T
            for zo in range(RUN):
                v1[pl.ds(zo * 32 + block * 16, 16)] = turned[zo * 16 : zo * 16 + 16]
        for i in range(1, RUN):
            to = lax.rem(z + i, RUN)
            remote(
                v1.at[aligned(to * 32, 32)], w1.at[aligned(z * 32, 32)], v_send.at[0], v_recv.at[0], z_peer(i)
            )
        w1[aligned(z * 32, 32)] = v1[aligned(z * 32, 32)]

    def forward_vectors():
        wait_bytes(w1.at[pl.ds(0, 7 * 32)], v_recv.at[0])
        for block in range(2):
            for q in range(16):
                v2[pl.ds((q // 2) * 32 + block * 16 + (q % 2) * 8, 8)] = w1[pl.ds(block * 16 + q, 8, stride=32), :]
        for i in range(1, RUN):
            to = lax.rem(g + i, RUN)
            remote(
                v2.at[aligned(to * 32, 32)], w2.at[aligned(g * 32, 32)], v_send.at[1], v_recv.at[1], g_peer(i)
            )
        w2[aligned(g * 32, 32)] = v2[aligned(g * 32, 32)]

    def take_vectors():
        wait_bytes(w2.at[pl.ds(0, 7 * 32)], v_recv.at[1])
        turned = [
            jnp.concatenate([w2[pl.ds(run * 32 + block * 16, 16)] for run in range(RUN)], axis=0).T
            for block in range(2)
        ]
        c_t[...] = turned[0][0:W]
        rhs_t[...] = turned[0][W : 2 * W]
        coup_t[...] = turned[1][0:W]

    loads[0].wait()
    for chunk in range(CHUNKS):
        pack(FWD, chunk)
        if chunk == 0:
            pl.semaphore_wait(barrier, 16)
        send_z(FWD, chunk)
    send_vectors()
    loads[4].wait()
    for chunk in range(CHUNKS):
        pack(BWD, chunk)
        if EAGER:
            send_z(BWD, chunk)
    for chunk in range(CHUNKS):
        pack(INV, chunk)
    for chunk in range(CHUNKS):
        forward_g(FWD, chunk)
    forward_vectors()
    if not EAGER:
        for chunk in range(CHUNKS):
            send_z(BWD, chunk)
    if EAGER > 1:
        for chunk in range(CHUNKS):
            send_z(INV, chunk)
    for chunk in range(CHUNKS):
        unpack(FWD, chunk)
    take_vectors()
    for level in range(3):
        compose(FWD, level)
        forward_g(BWD, level)
    c_t[...] = sweep(FWD, c_t[...])
    for chunk in range(CHUNKS):
        unpack(BWD, chunk)
    compose(BWD, 0)
    forward_g(INV, 0)
    compose(BWD, 1)
    compose(BWD, 2)
    forward_g(INV, 1)

    def stations_sum(turn, value):
        halo_out[turn] = value
        remote(halo_out.at[turn], halo_in.at[turn, 0], h_send.at[turn, 0], h_recv.at[turn, 0], up)
        remote(halo_out.at[turn], halo_in.at[turn, 1], h_send.at[turn, 1], h_recv.at[turn, 1], down)
        for side in range(2):
            wait_bytes(halo_in.at[turn, side], h_recv.at[turn, side])
            wait_bytes(halo_out.at[turn], h_send.at[turn, side])
        below = jnp.where(station > 0, halo_in[turn, 0], 0.0)
        above = jnp.where(station < 3, halo_in[turn, 1], 0.0)
        return below + above

    first[...] = sweep(BWD, c_t[...])
    middle[...] = rhs_t[...] - first[...] + coup_t[...] * stations_sum(0, first[...])
    forward_g(INV, 2)
    for chunk in range(CHUNKS):
        unpack(INV, chunk)
    vec[0:W] = middle[...]
    c_t[...] = sweep(FWD, matvec(lambda a: inv_t[pl.ds(a * W, W)], vec))
    second = sweep(BWD, c_t[...])
    c_t[...] = second
    stage[0, 0:W] = first[...] + second
    stage[0, W : 2 * W] = middle[...] - c_t[...] + coup_t[...] * stations_sum(1, c_t[...])

    o1[...] = stage[0].T

    for i in range(1, RUN):
        to = lax.rem(g + i, RUN)
        remote(o1.at[aligned(to * 16, 16)], p1.at[aligned(g * 16, 16)], v_send.at[2], v_recv.at[2], g_peer(i))
    p1[aligned(g * 16, 16)] = o1[aligned(g * 16, 16)]
    wait_bytes(p1.at[pl.ds(0, 7 * 16)], v_recv.at[2])
    for q in range(16):
        o2[pl.ds(q, 8, stride=16), :] = p1[pl.ds(q * 8, 8)]

    for i in range(1, RUN):
        to = lax.rem(z + i, RUN)
        remote(o2.at[aligned(to * 16, 16)], p2.at[aligned(z * 16, 16)], v_send.at[3], v_recv.at[3], z_peer(i))
    p2[aligned(z * 16, 16)] = o2[aligned(z * 16, 16)]
    wait_bytes(p2.at[pl.ds(0, 7 * 16)], v_recv.at[3])
    final = p2[...].T
    corr[...] = final[0:W]
    rem[...] = final[W : 2 * W]

    for kind in range(3):
        for chunk in range(CHUNKS):
            wait_bytes(s1.at[kind, pl.ds(0, 7 * CROWS)], mz_send.at[kind, chunk])
            wait_bytes(s2.at[kind, pl.ds(0, 7 * CROWS)], mg_send.at[kind, chunk])
    for at, ref in ((0, v1), (1, v2)):
        wait_bytes(ref.at[pl.ds(0, 7 * 32)], v_send.at[at])
    for at, ref in ((2, o1), (3, o2)):
        wait_bytes(ref.at[pl.ds(0, 7 * 16)], v_send.at[at])


def on_device(rhs, coupling, fwd_coupling, bwd_coupling, block_inverse):
    f32 = jnp.float32
    vmem = pl.BlockSpec(memory_space=pltpu.VMEM)
    dma = pltpu.SemaphoreType.DMA
    mat = pltpu.VMEM((3, W * W, L), f32)
    small = pltpu.VMEM((W, L), f32)
    square = pltpu.VMEM((L, L), f32)
    wide = pltpu.VMEM((2 * L, L), f32)
    corr, rem = pl.pallas_call(
        kernel,
        out_shape=(jax.ShapeDtypeStruct((W, L), f32),) * 2,
        in_specs=[pl.BlockSpec(memory_space=pl.ANY)] * 5,
        out_specs=(vmem, vmem),
        scratch_shapes=[
            small, small, pltpu.VMEM((3, W * W, L), jnp.bfloat16), dma((5,)),
            mat, pltpu.VMEM((3, W * W + ROWS, L), f32), mat, mat,
            pltpu.VMEM((2, 4, W * W, L), f32), pltpu.VMEM((W * W + 8, L), f32), pltpu.VMEM((W * W, L), f32),
            pltpu.VMEM((W + 8, L), f32), pltpu.VMEM((2, L, L), f32),
            wide, pltpu.VMEM((2 * L + 32, L), f32), wide, wide, square, square, pltpu.VMEM((L + 16, L), f32), square,
            pltpu.VMEM((2, W, L), f32), pltpu.VMEM((2, 2, W, L), f32),
            small, small, small, small, small,
            dma((3, CHUNKS)), dma((3, CHUNKS)), dma((3, CHUNKS)), dma((3, CHUNKS)),
            dma((4,)), dma((4,)), dma((2, 2)), dma((2, 2)),
        ],
        compiler_params=pltpu.CompilerParams(
            collective_id=0, has_side_effects=True, vmem_limit_bytes=62 << 20
        ),
        name="both_applies",
    )(
        rhs.reshape(W, L), coupling.reshape(W, L), fwd_coupling.reshape(W * W, L),
        bwd_coupling.reshape(W * W, L), block_inverse.reshape(W * W, L),
    )
    return corr.reshape(rhs.shape), rem.reshape(rhs.shape)


def solution(mesh):
    vector = P("azim", None, "axial", None)
    matrix = P("azim", None, None, "axial", None)
    return jax.shard_map(
        on_device,
        mesh=mesh,
        in_specs=(vector, vector, matrix, matrix, matrix),
        out_specs=(vector, vector),
        check_vma=False,
    )
```

```python
import functools

import jax
import jax.numpy as jnp
from jax import lax
from jax.experimental import pallas as pl
from jax.experimental.pallas import tpu as pltpu
from jax.sharding import PartitionSpec as P

MESH = pl.DeviceIdType.MESH
W = 48
L = 128
RUN = 8
PIECES = W * W // L
ROWS = PIECES * 16
PARTS = ((0, 9), (9, 6), (15, 3))
CHUNKS = len(PARTS)
FWD, BWD, INV = 0, 1, 2


def aligned(start, size):
    return pl.ds(start if isinstance(start, int) else pl.multiple_of(start, 8), size)


def part_rows(base, chunk):
    first, count = PARTS[chunk]
    return aligned(base + first * 16, count * 16)


def wait_bytes(ref, sem):
    pltpu.make_async_copy(ref, ref, sem).wait()


def matvec(load, vec_ref):
    acc = jnp.zeros((6, 8, L), jnp.float32)
    for a in range(W):
        acc = acc + load(a).reshape(6, 8, L) * vec_ref[pl.ds(a, 8, stride=0), :][None]
    return acc.reshape(W, L)


def kernel(
    rhs_in, coup_in, fwd_in, bwd_in, inv_in, corr, rem, rhs, coup, blocks, in_sem,
    s1, r1, s2, r2, maps, early, dup, packed, inv_t,
    vec, stage, turn, z_out, z_in, g_out, g_in, halo_out, halo_in,
    c_t, rhs_t, coup_t, first, middle,
    mz_send, mz_recv, mg_send, mg_recv, zv_send, zv_recv, gv_send, gv_recv, h_send, h_recv,
):
    me = lax.axis_index("azim")
    station = lax.axis_index("axial")
    z = lax.rem(me, RUN)
    g = me // RUN
    loads = [
        pltpu.make_async_copy(src, dst, in_sem.at[at])
        for at, (src, dst) in enumerate((
            (fwd_in, blocks.at[FWD]), (rhs_in, rhs), (coup_in, coup), (inv_in, blocks.at[INV]), (bwd_in, blocks.at[BWD]),
        ))
    ]
    for load in loads:
        load.start()

    def z_peer(i):
        return {"azim": g * RUN + lax.rem(z + i, RUN)}

    def g_peer(i):
        return {"azim": lax.rem(g + i, RUN) * RUN + z}

    up = {"axial": lax.rem(station + 1, 4)}
    down = {"axial": lax.rem(station + 3, 4)}

    lane = lax.broadcasted_iota(jnp.int32, (W, L), 1)
    lane_z = lax.rem(lane, RUN)
    lane_g = lane // 16

    barrier = pltpu.get_barrier_semaphore()

    def greet(i, _):
        pl.semaphore_signal(barrier, inc=1, device_id=z_peer(i), device_id_type=MESH)
        pl.semaphore_signal(barrier, inc=1, device_id=g_peer(i), device_id_type=MESH)
        return 0

    lax.fori_loop(1, RUN, greet, 0)
    pl.semaphore_signal(barrier, inc=1, device_id=up, device_id_type=MESH)
    pl.semaphore_signal(barrier, inc=1, device_id=down, device_id_type=MESH)

    def remote(src, dst, send, recv, device):
        pltpu.make_async_remote_copy(
            src_ref=src, dst_ref=dst, send_sem=send, recv_sem=recv,
            device_id=device, device_id_type=MESH,
        ).start()

    def pack(kind, chunk):
        def body(step, _):
            for inner in range(3):
                t = step * 3 + inner
                piece = blocks[kind, pl.ds(pl.multiple_of(t * L, L), L), :].astype(jnp.float32).T
                for zo in range(RUN):
                    s1[kind, aligned(zo * ROWS + t * 16, 16)] = piece[zo * 16 : zo * 16 + 16]
            return 0

        lax.fori_loop(PARTS[chunk][0] // 3, sum(PARTS[chunk]) // 3, body, 0)

    def send_z(kind, chunk):
        for i in range(1, RUN):
            to = lax.rem(z + i, RUN)
            remote(
                s1.at[kind, part_rows(to * ROWS, chunk)],
                r1.at[kind, part_rows(z * ROWS, chunk)],
                mz_send.at[kind, chunk], mz_recv.at[kind, chunk], z_peer(i),
            )
        own = part_rows(z * ROWS, chunk)
        r1[kind, own] = s1[kind, own]

    def forward_g(kind, chunk):
        wait_bytes(r1.at[kind, pl.ds(0, 7 * 16 * PARTS[chunk][1])], mz_recv.at[kind, chunk])

        def body(t, _):
            for q in range(16):
                s2[kind, aligned((q // 2) * ROWS + t * 16 + (q % 2) * 8, 8)] = r1[
                    kind, pl.ds(t * 16 + q, 8, stride=ROWS), :
                ]
            return 0

        lax.fori_loop(PARTS[chunk][0], sum(PARTS[chunk]), body, 0)
        send_g(kind, chunk)

    def pack_g(kind, chunk):
        def body(t, _):
            turn[0, 0:L] = blocks[kind, pl.ds(pl.multiple_of(t * L, L), L), :].astype(jnp.float32).T
            for q in range(16):
                s2[kind, aligned((q // 2) * ROWS + t * 16 + (q % 2) * 8, 8)] = turn[0, pl.ds(q, 8, stride=16), :]
            return 0

        lax.fori_loop(PARTS[chunk][0], sum(PARTS[chunk]), body, 0)
        send_g(kind, chunk)

    def send_g(kind, chunk):
        for i in range(1, RUN):
            to = lax.rem(g + i, RUN)
            remote(
                s2.at[kind, part_rows(to * ROWS, chunk)],
                r2.at[kind, part_rows(g * ROWS, chunk)],
                mg_send.at[kind, chunk], mg_recv.at[kind, chunk], g_peer(i),
            )
        own = part_rows(g * ROWS, chunk)
        r2[kind, own] = s2[kind, own]

    def unpack(kind, chunk):
        wait_bytes(r2.at[kind, pl.ds(0, 7 * 16 * PARTS[chunk][1])], mg_recv.at[kind, chunk])

        def body(step, _):
            for inner in range(3):
                t = step * 3 + inner
                rows = [r2[kind, aligned(run * ROWS + t * 16, 16)] for run in range(RUN)]
                piece = jnp.concatenate(rows, axis=0).T
                if kind == INV:
                    inv_t[pl.ds(pl.multiple_of(t * L, L), L), :] = piece
                else:
                    maps[kind, 0, pl.ds(pl.multiple_of(t * L, L), L), :] = -piece
            return 0

        lax.fori_loop(PARTS[chunk][0] // 3, sum(PARTS[chunk]) // 3, body, 0)

    def earlier(value, distance, kind):
        return pltpu.roll(value, distance if kind == FWD else L - distance, 1)

    def inside(distance, kind):
        return lane_z >= distance if kind == FWD else lane_z < RUN - distance

    def compose(kind, level):
        distance = 1 << level
        exists = inside(distance, kind)
        sub = lax.broadcasted_iota(jnp.int32, (W, L), 0)

        def shift(step, _):
            for inner in range(8):
                a = step * 8 + inner
                moved = earlier(maps[kind, level, aligned(a * W, W)], distance, kind)
                early[aligned(a * W, W)] = jnp.where(exists, moved, jnp.where(sub == a, 1.0, 0.0))
            return 0

        lax.fori_loop(0, W // 8, shift, 0)

        def product(four, _):
            acc = [jnp.zeros((6, 8, L), jnp.float32)] * 4
            for c in range(W):
                later = maps[kind, level, pl.ds(c * W, W)].reshape(6, 8, L)
                for i in range(4):
                    factor = early[pl.ds((four * 4 + i) * W + c, 8, stride=0), :]
                    acc[i] = acc[i] + later * factor[None]
            for i in range(4):
                maps[kind, level + 1, aligned((four * 4 + i) * W, W)] = acc[i].reshape(W, L)
            return 0

        lax.fori_loop(0, W // 4, product, 0)

    even = lane_z % 2 == 0
    low2 = lane_z % 4 < 2
    low4 = lane_z < 4
    share = (0, 24, 12, 36)

    def back(value, distance):
        return pltpu.roll(value, L - distance, 1)

    def ahead(value, distance):
        return pltpu.roll(value, distance, 1)

    def rows_of(ref, a):
        return ref[aligned(a * W, W)]

    def each(start, stop, width, do):
        def body(step, _):
            for inner in range(width):
                do(step * width + inner)
            return 0

        lax.fori_loop(start // width, stop // width, body, 0)

    def packed_product(start, stop, width, over, more=False):
        def body(step, _):
            places = [aligned((step * width + i) * W, W) for i in range(width)]
            zero = jnp.zeros((6, 8, L), jnp.float32)
            acc = [packed[place].reshape(6, 8, L) if more else zero for place in places]
            for c in over:
                later = dup[pl.ds(c * W, W)].reshape(6, 8, L)
                for i in range(width):
                    factor = early[pl.ds((step * width + i) * W + c, 8, stride=0), :]
                    acc[i] = acc[i] + later * factor[None]
            for i in range(width):
                packed[places[i]] = acc[i].reshape(W, L)
            return 0

        lax.fori_loop(start // width, stop // width, body, 0)

    one, two, four, eight = (maps.at[BWD, level] for level in range(4))

    def early_pair(a):
        early[aligned(a * W, W)] = jnp.where(even, back(rows_of(one, a), 1), rows_of(one, a + 24))

    def later_pair(c):
        value = rows_of(one, c)
        dup[aligned(c * W, W)] = jnp.where(even, value, ahead(value, 1))

    def tree_start():
        each(0, 16, 8, early_pair)
        each(0, 40, 8, later_pair)
        packed_product(0, 16, 4, range(40))

    def tree_rest():
        each(16, 24, 8, early_pair)
        each(40, 48, 8, later_pair)
        packed_product(0, 16, 4, range(40, 48), True)
        packed_product(16, 24, 4, range(48))

        def early_quad(a):
            early[aligned(a * W, W)] = jnp.where(low2, back(rows_of(packed, a), 2), rows_of(packed, a + 12))

        def full_pair(a):
            value = rows_of(packed, a)
            for at, full in ((a, jnp.where(even, value, ahead(value, 1))), (a + 24, jnp.where(even, back(value, 1), value))):
                two[aligned(at * W, W)] = full
                dup[aligned(at * W, W)] = jnp.where(low2, full, ahead(full, 2))

        each(0, 12, 6, early_quad)
        each(0, 24, 4, full_pair)
        packed_product(0, 12, 4, range(48))

        def early_eight(a):
            early[aligned(a * W, W)] = jnp.where(low4, back(rows_of(packed, a), 4), rows_of(packed, a + 6))

        def full_quad(a):
            value = rows_of(packed, a)
            evens = jnp.where(even, value, ahead(value, 1))
            odds = jnp.where(even, back(value, 1), value)
            for q, pair in enumerate((evens, odds, evens, odds)):
                full = jnp.where(low2, pair, ahead(pair, 2)) if q < 2 else jnp.where(low2, back(pair, 2), pair)
                four[aligned((a + share[q]) * W, W)] = full
                dup[aligned((a + share[q]) * W, W)] = jnp.where(low4, full, ahead(full, 4))

        each(0, 6, 6, early_eight)
        each(0, 12, 2, full_quad)
        packed_product(0, 6, 3, range(48))

        def full_eight(a):
            value = rows_of(packed, a)
            for zz in range(RUN):
                full = back(value, zz) if zz else value
                at = a + share[zz % 4] + (6 if zz >= 4 else 0)
                eight[aligned(at * W, W)] = jnp.where(lane_z == 4, rows_of(four, at), full)

        each(0, 6, 2, full_eight)

    def tree_sweep(value):
        def add(state, level, entering):
            vec[0:W] = entering
            return state + apply_map(BWD, level)

        state = add(value, 0, jnp.where(even, back(value, 1), 0.0))
        state = add(state, 1, jnp.where(lane_z % 4 == 0, back(state, 2), 0.0))
        state = add(state, 2, jnp.where(lane_z == 0, back(state, 4), 0.0))

        def run_step(n, carry):
            running, entering = carry
            moved = jnp.where(lane_z == 0, back(running, 16), 0.0)
            entering = jnp.where(RUN - 1 - lane_g == n - RUN, moved, entering)
            return add(state, 3, moved), entering

        running, entering = lax.fori_loop(1, 15, run_step, (state, jnp.zeros((W, L), jnp.float32)))
        entering = jnp.where(lane_g == 0, back(running, 16), entering)
        entering = jnp.where(lane_z == 0, entering, 0.0)
        at_four, at_six, at_seven = (ahead(entering, d) for d in (4, 6, 7))
        state = add(state, 3, entering + at_four)
        state = add(state, 1, jnp.where(lane_z == 2, back(state, 2), at_six))
        return add(state, 0, jnp.where(even, 0.0, jnp.where(lane_z == 7, at_seven, back(state, 1))))

    def apply_map(kind, level):
        return matvec(lambda a: maps[kind, level, pl.ds(a * W, W)], vec)

    def sweep(kind, value):
        state = value
        for level in range(3):
            distance = 1 << level
            moved = earlier(state, distance, kind)
            vec[0:W] = jnp.where(inside(distance, kind), moved, 0.0)
            state = state + apply_map(kind, level)
        order = lane_g if kind == FWD else RUN - 1 - lane_g

        def run_step(n, carry):
            running, entering = carry
            moved = earlier(running, 16, kind)
            entering = jnp.where(order == n - RUN, moved, entering)
            vec[0:W] = moved
            return state + apply_map(kind, 3), entering

        running, entering = lax.fori_loop(1, 15, run_step, (state, jnp.zeros((W, L), jnp.float32)))
        entering = jnp.where(order == RUN - 1, earlier(running, 16, kind), entering)
        place = RUN - 1 - lane_z if kind == FWD else lane_z
        for distance in (1, 2, 4):
            back = pltpu.roll(entering, L - distance if kind == FWD else distance, 1)
            entering = jnp.where(place < distance, entering, back)
        vec[0:W] = entering
        return state + apply_map(kind, 3)

    def g_stage(at, gather):
        for run in range(RUN):
            for half in range(2):
                g_out[at, run * 16 + half * 8 : run * 16 + half * 8 + 8] = gather(run, half)
        for i in range(1, RUN):
            to = lax.rem(g + i, RUN)
            remote(
                g_out.at[at, aligned(to * 16, 16)], g_in.at[at, aligned(g * 16, 16)],
                gv_send.at[at], gv_recv.at[at], g_peer(i),
            )
        g_in[at, aligned(g * 16, 16)] = g_out[at, aligned(g * 16, 16)]

    def z_start(at, value):
        stage[0:W] = value
        turn[0, 0:L] = stage[...].T
        for zz in range(RUN):
            for half in range(2):
                z_out[at, pl.ds(zz * 16 + half * 8, 8)] = turn[0, pl.ds(zz + 64 * half, 8, stride=8), :]
        for i in (4, 3, 5, 2, 6, 1, 7):
            to = lax.rem(z + i, RUN)
            remote(
                z_out.at[at, aligned(to * 16, 16)], z_in.at[at, aligned(z * 16, 16)],
                zv_send.at[at], zv_recv.at[at], z_peer(i),
            )
        z_in[at, aligned(z * 16, 16)] = z_out[at, aligned(z * 16, 16)]

    def z_finish(at):
        wait_bytes(z_in.at[at, pl.ds(0, 7 * 16)], zv_recv.at[at])
        for m in range(16):
            turn[0, m * 8 : m * 8 + 8] = z_in[at, pl.ds(m, 8, stride=16), :]
        return turn[0, 0:L].T[0:W]

    def stations_start(at, value):
        halo_out[at] = value
        remote(halo_out.at[at], halo_in.at[at, 0], h_send.at[at, 0], h_recv.at[at, 0], up)
        remote(halo_out.at[at], halo_in.at[at, 1], h_send.at[at, 1], h_recv.at[at, 1], down)

    def stations_finish(at):
        for side in range(2):
            wait_bytes(halo_in.at[at, side], h_recv.at[at, side])
            wait_bytes(halo_out.at[at], h_send.at[at, side])
        below = jnp.where(station > 0, halo_in[at, 0], 0.0)
        above = jnp.where(station < 3, halo_in[at, 1], 0.0)
        return below + above

    def inverse(ref):
        return matvec(lambda a: inv_t[pl.ds(a * W, W)], ref)

    loads[0].wait()
    for chunk in range(CHUNKS):
        pack(FWD, chunk)
        if chunk == 0:
            pl.semaphore_wait(barrier, 16)
        send_z(FWD, chunk)
    for load in loads[1:]:
        load.wait()
    vec[0:W] = rhs[...]
    stage[...] = jnp.zeros((L, L), jnp.float32)
    stage[0:W] = matvec(lambda a: blocks[INV, pl.ds(a * W, W), :].astype(jnp.float32), vec)
    stage[W : 2 * W] = rhs[...]
    turn[0, 0:L] = stage[...].T
    g_stage(0, lambda run, half: turn[0, pl.ds(run * 2 + half, 8, stride=16), :])
    stage[0:W] = coup[...]
    turn[1, 0:L] = stage[...].T
    g_stage(2, lambda run, half: turn[1, pl.ds(run * 2 + half, 8, stride=16), :])
    for chunk in range(CHUNKS):
        pack(BWD, chunk)
    wait_bytes(g_in.at[0, pl.ds(0, 7 * 16)], gv_recv.at[0])
    turned = g_in[0].T
    rhs_t[...] = turned[W : 2 * W]
    z_start(0, turned[0:W])
    for chunk in range(CHUNKS):
        pack_g(INV, chunk)
    for chunk in range(CHUNKS):
        send_z(BWD, chunk)
    for chunk in range(CHUNKS):
        forward_g(FWD, chunk)
    for chunk in range(CHUNKS):
        unpack(FWD, chunk)
    compose(FWD, 0)
    compose(FWD, 1)
    forward_g(BWD, 0)
    wait_bytes(g_in.at[2, pl.ds(0, 7 * 16)], gv_recv.at[2])
    coup_t[...] = g_in[2].T[0:W]
    for chunk in range(CHUNKS):
        unpack(INV, chunk)
    compose(FWD, 2)
    c_t[...] = z_finish(0)
    c_t[...] = sweep(FWD, c_t[...])
    forward_g(BWD, 1)
    forward_g(BWD, 2)
    unpack(BWD, 0)
    unpack(BWD, 1)
    tree_start()
    unpack(BWD, 2)
    tree_rest()

    z_start(1, tree_sweep(c_t[...]))
    first[...] = z_finish(1)
    stations_start(0, first[...])
    vec[0:W] = rhs_t[...] - first[...] + coup_t[...] * stations_finish(0)
    middle[...] = vec[0:W]
    z_start(2, inverse(vec))
    c_t[...] = z_finish(2)
    c_t[...] = sweep(FWD, c_t[...])
    z_start(3, tree_sweep(c_t[...]))
    c_t[...] = z_finish(3)
    stations_start(1, c_t[...])
    stage[0:W] = first[...] + c_t[...]
    stage[W : 2 * W] = middle[...] - c_t[...] + coup_t[...] * stations_finish(1)
    turn[0, 0:L] = stage[...].T
    g_stage(1, lambda run, half: turn[0, pl.ds(run * 16 + half * 8, 8)])
    wait_bytes(g_in.at[1, pl.ds(0, 7 * 16)], gv_recv.at[1])
    for q in range(16):
        turn[1, pl.ds(q, 8, stride=16), :] = g_in[1, pl.ds(q * 8, 8)]
    final = turn[1, 0:L].T
    corr[...] = final[0:W]
    rem[...] = final[W : 2 * W]

    for kind in range(3):
        for chunk in range(CHUNKS):
            if kind != INV:
                wait_bytes(s1.at[kind, pl.ds(0, 7 * 16 * PARTS[chunk][1])], mz_send.at[kind, chunk])
            wait_bytes(s2.at[kind, pl.ds(0, 7 * 16 * PARTS[chunk][1])], mg_send.at[kind, chunk])
    for at in range(4):
        wait_bytes(z_out.at[at, pl.ds(0, 7 * 16)], zv_send.at[at])
    for at in range(3):
        wait_bytes(g_out.at[at, pl.ds(0, 7 * 16)], gv_send.at[at])


def on_device(rhs, coupling, fwd_coupling, bwd_coupling, block_inverse):
    f32 = jnp.float32
    vmem = pl.BlockSpec(memory_space=pltpu.VMEM)
    dma = pltpu.SemaphoreType.DMA
    mat = pltpu.VMEM((3, W * W, L), f32)
    small = pltpu.VMEM((W, L), f32)
    corr, rem = pl.pallas_call(
        kernel,
        out_shape=(jax.ShapeDtypeStruct((W, L), f32),) * 2,
        in_specs=[pl.BlockSpec(memory_space=pl.ANY)] * 5,
        out_specs=(vmem, vmem),
        scratch_shapes=[
            small, small, pltpu.VMEM((3, W * W, L), jnp.bfloat16), dma((5,)),
            pltpu.VMEM((2, W * W, L), f32), pltpu.VMEM((2, W * W + ROWS, L), f32), mat, mat,
            pltpu.VMEM((2, 4, W * W, L), f32), pltpu.VMEM((W * W + 8, L), f32), pltpu.VMEM((W * W, L), f32),
            pltpu.VMEM((W * W // 2, L), f32), pltpu.VMEM((W * W, L), f32),
            pltpu.VMEM((W + 8, L), f32), pltpu.VMEM((L, L), f32), pltpu.VMEM((2, L + 16, L), f32),
            pltpu.VMEM((4, L, L), f32), pltpu.VMEM((4, L + 16, L), f32),
            pltpu.VMEM((3, L, L), f32), pltpu.VMEM((3, L, L), f32),
            pltpu.VMEM((2, W, L), f32), pltpu.VMEM((2, 2, W, L), f32),
            small, small, small, small, small,
            dma((2, CHUNKS)), dma((2, CHUNKS)), dma((3, CHUNKS)), dma((3, CHUNKS)),
            dma((4,)), dma((4,)), dma((3,)), dma((3,)), dma((2, 2)), dma((2, 2)),
        ],
        compiler_params=pltpu.CompilerParams(
            collective_id=0, has_side_effects=True, vmem_limit_bytes=62 << 20
        ),
        name="both_applies",
    )(
        rhs.reshape(W, L), coupling.reshape(W, L), fwd_coupling.reshape(W * W, L),
        bwd_coupling.reshape(W * W, L), block_inverse.reshape(W * W, L),
    )
    return corr.reshape(rhs.shape), rem.reshape(rhs.shape)


def solution(mesh):
    vector = P("azim", None, "axial", None)
    matrix = P("azim", None, None, "axial", None)
    return jax.shard_map(
        on_device,
        mesh=mesh,
        in_specs=(vector, vector, matrix, matrix, matrix),
        out_specs=(vector, vector),
        check_vma=False,
    )
```

```python
import functools

import jax
import jax.numpy as jnp
from jax import lax
from jax.experimental import pallas as pl
from jax.experimental.pallas import tpu as pltpu
from jax.sharding import PartitionSpec as P

MESH = pl.DeviceIdType.MESH
W = 48
L = 128
RUN = 8
PIECES = W * W // L
ROWS = PIECES * 16
PARTS = ((0, 9), (9, 6), (15, 3))
CHUNKS = len(PARTS)
FWD, BWD, INV = 0, 1, 2


def aligned(start, size):
    return pl.ds(start if isinstance(start, int) else pl.multiple_of(start, 8), size)


def part_rows(base, chunk):
    first, count = PARTS[chunk]
    return aligned(base + first * 16, count * 16)


def wait_bytes(ref, sem):
    pltpu.make_async_copy(ref, ref, sem).wait()


def matvec(load, vec_ref):
    acc = jnp.zeros((6, 8, L), jnp.float32)
    for a in range(W):
        acc = acc + load(a).reshape(6, 8, L) * vec_ref[pl.ds(a, 8, stride=0), :][None]
    return acc.reshape(W, L)


def kernel(
    rhs_in, coup_in, fwd_in, bwd_in, inv_in, lines, rhs, coup, blocks, in_sem,
    s1, r1, s2, r2, maps, early, dup, packed, inv_t,
    vec, stage, turn, z_out, z_in, g_out, g_in, halo_out, halo_in,
    c_t, rhs_t, coup_t, first, middle,
    mz_send, mz_recv, mg_send, mg_recv, zv_send, zv_recv, gv_send, gv_recv, h_send, h_recv,
):
    me = lax.axis_index("azim")
    station = lax.axis_index("axial")
    z = lax.rem(me, RUN)
    g = me // RUN
    loads = [
        pltpu.make_async_copy(src, dst, in_sem.at[at])
        for at, (src, dst) in enumerate((
            (fwd_in, blocks.at[FWD]), (rhs_in, rhs), (coup_in, coup), (inv_in, blocks.at[INV]), (bwd_in, blocks.at[BWD]),
        ))
    ]
    for load in loads:
        load.start()

    def z_peer(i):
        return {"azim": g * RUN + lax.rem(z + i, RUN)}

    def g_peer(i):
        return {"azim": lax.rem(g + i, RUN) * RUN + z}

    up = {"axial": lax.rem(station + 1, 4)}
    down = {"axial": lax.rem(station + 3, 4)}

    lane = lax.broadcasted_iota(jnp.int32, (W, L), 1)
    lane_z = lax.rem(lane, RUN)
    lane_g = lane // 16

    barrier = pltpu.get_barrier_semaphore()

    def greet(i, _):
        pl.semaphore_signal(barrier, inc=1, device_id=z_peer(i), device_id_type=MESH)
        pl.semaphore_signal(barrier, inc=1, device_id=g_peer(i), device_id_type=MESH)
        return 0

    lax.fori_loop(1, RUN, greet, 0)
    pl.semaphore_signal(barrier, inc=1, device_id=up, device_id_type=MESH)
    pl.semaphore_signal(barrier, inc=1, device_id=down, device_id_type=MESH)

    def remote(src, dst, send, recv, device):
        pltpu.make_async_remote_copy(
            src_ref=src, dst_ref=dst, send_sem=send, recv_sem=recv,
            device_id=device, device_id_type=MESH,
        ).start()

    def pack(kind, chunk):
        def body(step, _):
            for inner in range(3):
                t = step * 3 + inner
                piece = blocks[kind, pl.ds(pl.multiple_of(t * L, L), L), :].astype(jnp.float32).T
                for zo in range(RUN):
                    s1[kind, aligned(zo * ROWS + t * 16, 16)] = piece[zo * 16 : zo * 16 + 16]
            return 0

        lax.fori_loop(PARTS[chunk][0] // 3, sum(PARTS[chunk]) // 3, body, 0)

    def send_z(kind, chunk):
        for i in range(1, RUN):
            to = lax.rem(z + i, RUN)
            remote(
                s1.at[kind, part_rows(to * ROWS, chunk)],
                r1.at[kind, part_rows(z * ROWS, chunk)],
                mz_send.at[kind, chunk], mz_recv.at[kind, chunk], z_peer(i),
            )
        own = part_rows(z * ROWS, chunk)
        r1[kind, own] = s1[kind, own]

    def forward_g(kind, chunk):
        wait_bytes(r1.at[kind, pl.ds(0, 7 * 16 * PARTS[chunk][1])], mz_recv.at[kind, chunk])

        def body(t, _):
            for q in range(16):
                s2[kind, aligned((q // 2) * ROWS + t * 16 + (q % 2) * 8, 8)] = r1[
                    kind, pl.ds(t * 16 + q, 8, stride=ROWS), :
                ]
            return 0

        lax.fori_loop(PARTS[chunk][0], sum(PARTS[chunk]), body, 0)
        send_g(kind, chunk)

    def pack_g(kind, chunk):
        def body(t, _):
            turn[0, 0:L] = blocks[kind, pl.ds(pl.multiple_of(t * L, L), L), :].astype(jnp.float32).T
            for q in range(16):
                s2[kind, aligned((q // 2) * ROWS + t * 16 + (q % 2) * 8, 8)] = turn[0, pl.ds(q, 8, stride=16), :]
            return 0

        lax.fori_loop(PARTS[chunk][0], sum(PARTS[chunk]), body, 0)
        send_g(kind, chunk)

    def send_g(kind, chunk):
        for i in range(1, RUN):
            to = lax.rem(g + i, RUN)
            remote(
                s2.at[kind, part_rows(to * ROWS, chunk)],
                r2.at[kind, part_rows(g * ROWS, chunk)],
                mg_send.at[kind, chunk], mg_recv.at[kind, chunk], g_peer(i),
            )
        own = part_rows(g * ROWS, chunk)
        r2[kind, own] = s2[kind, own]

    def unpack(kind, chunk):
        wait_bytes(r2.at[kind, pl.ds(0, 7 * 16 * PARTS[chunk][1])], mg_recv.at[kind, chunk])

        def body(step, _):
            for inner in range(3):
                t = step * 3 + inner
                rows = [r2[kind, aligned(run * ROWS + t * 16, 16)] for run in range(RUN)]
                piece = jnp.concatenate(rows, axis=0).T
                if kind == INV:
                    inv_t[pl.ds(pl.multiple_of(t * L, L), L), :] = piece
                else:
                    maps[kind, 0, pl.ds(pl.multiple_of(t * L, L), L), :] = -piece
            return 0

        lax.fori_loop(PARTS[chunk][0] // 3, sum(PARTS[chunk]) // 3, body, 0)

    def earlier(value, distance, kind):
        return pltpu.roll(value, distance if kind == FWD else L - distance, 1)

    def inside(distance, kind):
        if distance >= 16:
            return lane_g >= distance // 16
        return lane_z >= distance if kind == FWD else lane_z < RUN - distance

    def compose(kind, level):
        distance = 1 << level if level < 3 else 16 << (level - 3)
        exists = inside(distance, kind)
        sub = lax.broadcasted_iota(jnp.int32, (W, L), 0)

        def shift(step, _):
            for inner in range(8):
                a = step * 8 + inner
                moved = earlier(maps[kind, level, aligned(a * W, W)], distance, kind)
                early[aligned(a * W, W)] = jnp.where(exists, moved, jnp.where(sub == a, 1.0, 0.0))
            return 0

        lax.fori_loop(0, W // 8, shift, 0)

        def product(four, _):
            acc = [jnp.zeros((6, 8, L), jnp.float32)] * 4
            for c in range(W):
                later = maps[kind, level, pl.ds(c * W, W)].reshape(6, 8, L)
                for i in range(4):
                    factor = early[pl.ds((four * 4 + i) * W + c, 8, stride=0), :]
                    acc[i] = acc[i] + later * factor[None]
            for i in range(4):
                maps[kind, level + 1, aligned((four * 4 + i) * W, W)] = acc[i].reshape(W, L)
            return 0

        lax.fori_loop(0, W // 4, product, 0)

    def paired_sweep(value):
        def add(state, level, entering):
            vec[0:W] = entering
            return state + apply_map(FWD, level)

        def moved(state, distance):
            return jnp.where(inside(distance, FWD), pltpu.roll(state, distance, 1), 0.0)

        state = value
        for level in range(3):
            state = add(state, level, moved(state, 1 << level))
        two_runs = add(state, 3, moved(state, 16))
        four_runs = add(two_runs, 4, moved(two_runs, 32))
        turn_end = pltpu.roll(add(four_runs, 5, moved(four_runs, 64)), 16, 1)
        wrapped = turn_end
        for runs in (1, 2, 4):
            wrapped = jnp.where(lane_g < runs, wrapped, pltpu.roll(wrapped, 16 * runs, 1))
        low = add(four_runs, 5, wrapped)
        high = add(four_runs, 5, pltpu.roll(low, 64, 1))
        leaving = jnp.where(lane_g < 4, low, high)
        entering = jnp.where(lane_g == 0, turn_end, pltpu.roll(leaving, 16, 1))
        for distance in (1, 2, 4):
            entering = jnp.where(RUN - 1 - lane_z < distance, entering, pltpu.roll(entering, L - distance, 1))
        return add(state, 3, entering)

    even = lane_z % 2 == 0
    low2 = lane_z % 4 < 2
    low4 = lane_z < 4
    share = (0, 24, 12, 36)

    def back(value, distance):
        return pltpu.roll(value, L - distance, 1)

    def ahead(value, distance):
        return pltpu.roll(value, distance, 1)

    def rows_of(ref, a):
        return ref[aligned(a * W, W)]

    def each(start, stop, width, do):
        def body(step, _):
            for inner in range(width):
                do(step * width + inner)
            return 0

        lax.fori_loop(start // width, stop // width, body, 0)

    def packed_product(start, stop, width, over, more=False):
        def body(step, _):
            places = [aligned((step * width + i) * W, W) for i in range(width)]
            zero = jnp.zeros((6, 8, L), jnp.float32)
            acc = [packed[place].reshape(6, 8, L) if more else zero for place in places]
            for c in over:
                later = dup[pl.ds(c * W, W)].reshape(6, 8, L)
                for i in range(width):
                    factor = early[pl.ds((step * width + i) * W + c, 8, stride=0), :]
                    acc[i] = acc[i] + later * factor[None]
            for i in range(width):
                packed[places[i]] = acc[i].reshape(W, L)
            return 0

        lax.fori_loop(start // width, stop // width, body, 0)

    one, two, four, eight = (maps.at[BWD, level] for level in range(4))

    def early_pair(a):
        early[aligned(a * W, W)] = jnp.where(even, back(rows_of(one, a), 1), rows_of(one, a + 24))

    def later_pair(c):
        value = rows_of(one, c)
        dup[aligned(c * W, W)] = jnp.where(even, value, ahead(value, 1))

    def tree_start():
        each(0, 16, 8, early_pair)
        each(0, 40, 8, later_pair)
        packed_product(0, 16, 4, range(40))

    def tree_rest():
        each(16, 24, 8, early_pair)
        each(40, 48, 8, later_pair)
        packed_product(0, 16, 4, range(40, 48), True)
        packed_product(16, 24, 4, range(48))

        def early_quad(a):
            early[aligned(a * W, W)] = jnp.where(low2, back(rows_of(packed, a), 2), rows_of(packed, a + 12))

        def full_pair(a):
            value = rows_of(packed, a)
            for at, full in ((a, jnp.where(even, value, ahead(value, 1))), (a + 24, jnp.where(even, back(value, 1), value))):
                two[aligned(at * W, W)] = full
                dup[aligned(at * W, W)] = jnp.where(low2, full, ahead(full, 2))

        each(0, 12, 6, early_quad)
        each(0, 24, 4, full_pair)
        packed_product(0, 12, 4, range(48))

        def early_eight(a):
            early[aligned(a * W, W)] = jnp.where(low4, back(rows_of(packed, a), 4), rows_of(packed, a + 6))

        def full_quad(a):
            value = rows_of(packed, a)
            evens = jnp.where(even, value, ahead(value, 1))
            odds = jnp.where(even, back(value, 1), value)
            for q, pair in enumerate((evens, odds, evens, odds)):
                full = jnp.where(low2, pair, ahead(pair, 2)) if q < 2 else jnp.where(low2, back(pair, 2), pair)
                four[aligned((a + share[q]) * W, W)] = full
                dup[aligned((a + share[q]) * W, W)] = jnp.where(low4, full, ahead(full, 4))

        each(0, 6, 6, early_eight)
        each(0, 12, 2, full_quad)
        packed_product(0, 6, 3, range(48))

        def full_eight(a):
            value = rows_of(packed, a)
            for zz in range(RUN):
                full = back(value, zz) if zz else value
                at = a + share[zz % 4] + (6 if zz >= 4 else 0)
                eight[aligned(at * W, W)] = jnp.where(lane_z == 4, rows_of(four, at), full)

        each(0, 6, 2, full_eight)

    def tree_sweep(value):
        def add(state, level, entering):
            vec[0:W] = entering
            return state + apply_map(BWD, level)

        state = add(value, 0, jnp.where(even, back(value, 1), 0.0))
        state = add(state, 1, jnp.where(lane_z % 4 == 0, back(state, 2), 0.0))
        state = add(state, 2, jnp.where(lane_z == 0, back(state, 4), 0.0))

        def run_step(n, carry):
            running, entering = carry
            moved = jnp.where(lane_z == 0, back(running, 16), 0.0)
            entering = jnp.where(RUN - 1 - lane_g == n - RUN, moved, entering)
            return add(state, 3, moved), entering

        running, entering = lax.fori_loop(1, 15, run_step, (state, jnp.zeros((W, L), jnp.float32)))
        entering = jnp.where(lane_g == 0, back(running, 16), entering)
        entering = jnp.where(lane_z == 0, entering, 0.0)
        at_four, at_six, at_seven = (ahead(entering, d) for d in (4, 6, 7))
        state = add(state, 3, entering + at_four)
        state = add(state, 1, jnp.where(lane_z == 2, back(state, 2), at_six))
        return add(state, 0, jnp.where(even, 0.0, jnp.where(lane_z == 7, at_seven, back(state, 1))))

    def apply_map(kind, level):
        return matvec(lambda a: maps[kind, level, pl.ds(a * W, W)], vec)

    def sweep(kind, value):
        state = value
        for level in range(3):
            distance = 1 << level
            moved = earlier(state, distance, kind)
            vec[0:W] = jnp.where(inside(distance, kind), moved, 0.0)
            state = state + apply_map(kind, level)
        order = lane_g if kind == FWD else RUN - 1 - lane_g

        def run_step(n, carry):
            running, entering = carry
            moved = earlier(running, 16, kind)
            entering = jnp.where(order == n - RUN, moved, entering)
            vec[0:W] = moved
            return state + apply_map(kind, 3), entering

        running, entering = lax.fori_loop(1, 15, run_step, (state, jnp.zeros((W, L), jnp.float32)))
        entering = jnp.where(order == RUN - 1, earlier(running, 16, kind), entering)
        place = RUN - 1 - lane_z if kind == FWD else lane_z
        for distance in (1, 2, 4):
            back = pltpu.roll(entering, L - distance if kind == FWD else distance, 1)
            entering = jnp.where(place < distance, entering, back)
        vec[0:W] = entering
        return state + apply_map(kind, 3)

    def g_stage(at, gather):
        for run in range(RUN):
            for half in range(2):
                g_out[at, run * 16 + half * 8 : run * 16 + half * 8 + 8] = gather(run, half)
        for i in range(1, RUN):
            to = lax.rem(g + i, RUN)
            remote(
                g_out.at[at, aligned(to * 16, 16)], g_in.at[at, aligned(g * 16, 16)],
                gv_send.at[at], gv_recv.at[at], g_peer(i),
            )
        g_in[at, aligned(g * 16, 16)] = g_out[at, aligned(g * 16, 16)]

    def z_start(at, value):
        stage[0:W] = value
        turn[0, 0:L] = stage[...].T
        for zz in range(RUN):
            for half in range(2):
                z_out[at, pl.ds(zz * 16 + half * 8, 8)] = turn[0, pl.ds(zz + 64 * half, 8, stride=8), :]
        for i in (4, 3, 5, 2, 6, 1, 7):
            to = lax.rem(z + i, RUN)
            remote(
                z_out.at[at, aligned(to * 16, 16)], z_in.at[at, aligned(z * 16, 16)],
                zv_send.at[at], zv_recv.at[at], z_peer(i),
            )
        z_in[at, aligned(z * 16, 16)] = z_out[at, aligned(z * 16, 16)]

    def z_finish(at):
        wait_bytes(z_in.at[at, pl.ds(0, 7 * 16)], zv_recv.at[at])
        for m in range(16):
            turn[0, m * 8 : m * 8 + 8] = z_in[at, pl.ds(m, 8, stride=16), :]
        return turn[0, 0:L].T[0:W]

    def stations_start(at, value):
        halo_out[at] = value
        remote(halo_out.at[at], halo_in.at[at, 0], h_send.at[at, 0], h_recv.at[at, 0], up)
        remote(halo_out.at[at], halo_in.at[at, 1], h_send.at[at, 1], h_recv.at[at, 1], down)

    def stations_finish(at):
        for side in range(2):
            wait_bytes(halo_in.at[at, side], h_recv.at[at, side])
            wait_bytes(halo_out.at[at], h_send.at[at, side])
        below = jnp.where(station > 0, halo_in[at, 0], 0.0)
        above = jnp.where(station < 3, halo_in[at, 1], 0.0)
        return below + above

    def inverse(ref):
        return matvec(lambda a: inv_t[pl.ds(a * W, W)], ref)

    loads[0].wait()
    for chunk in range(CHUNKS):
        pack(FWD, chunk)
        if chunk == 0:
            pl.semaphore_wait(barrier, 16)
        send_z(FWD, chunk)
    for load in loads[1:]:
        load.wait()
    vec[0:W] = rhs[...]
    stage[...] = jnp.zeros((L, L), jnp.float32)
    stage[0:W] = matvec(lambda a: blocks[INV, pl.ds(a * W, W), :].astype(jnp.float32), vec)
    stage[W : 2 * W] = rhs[...]
    turn[0, 0:L] = stage[...].T
    g_stage(0, lambda run, half: turn[0, pl.ds(run * 2 + half, 8, stride=16), :])
    stage[0:W] = coup[...]
    turn[1, 0:L] = stage[...].T
    g_stage(2, lambda run, half: turn[1, pl.ds(run * 2 + half, 8, stride=16), :])
    for chunk in range(CHUNKS):
        pack(BWD, chunk)
    wait_bytes(g_in.at[0, pl.ds(0, 7 * 16)], gv_recv.at[0])
    turned = g_in[0].T
    rhs_t[...] = turned[W : 2 * W]
    z_start(0, turned[0:W])
    for chunk in range(CHUNKS):
        pack_g(INV, chunk)
    for chunk in range(CHUNKS):
        send_z(BWD, chunk)
    for chunk in range(CHUNKS):
        forward_g(FWD, chunk)
    for chunk in range(CHUNKS):
        unpack(FWD, chunk)
    compose(FWD, 0)
    compose(FWD, 1)
    forward_g(BWD, 0)
    wait_bytes(g_in.at[2, pl.ds(0, 7 * 16)], gv_recv.at[2])
    coup_t[...] = g_in[2].T[0:W]
    for chunk in range(CHUNKS):
        unpack(INV, chunk)
    compose(FWD, 2)
    c_t[...] = z_finish(0)
    c_t[...] = sweep(FWD, c_t[...])
    forward_g(BWD, 1)
    forward_g(BWD, 2)
    unpack(BWD, 0)
    unpack(BWD, 1)
    tree_start()
    unpack(BWD, 2)
    tree_rest()

    z_start(1, tree_sweep(c_t[...]))
    compose(FWD, 3)
    first[...] = z_finish(1)
    stations_start(0, first[...])
    vec[0:W] = rhs_t[...] - first[...] + coup_t[...] * stations_finish(0)
    middle[...] = vec[0:W]
    z_start(2, inverse(vec))
    compose(FWD, 4)
    c_t[...] = z_finish(2)
    c_t[...] = paired_sweep(c_t[...])
    z_start(3, tree_sweep(c_t[...]))
    c_t[...] = z_finish(3)
    stations_start(1, c_t[...])
    stage[0:W] = first[...] + c_t[...]
    stage[W : 2 * W] = middle[...] - c_t[...] + coup_t[...] * stations_finish(1)
    turn[0, 0:L] = stage[...].T
    g_stage(1, lambda run, half: turn[0, pl.ds(run * 16 + half * 8, 8)])
    wait_bytes(g_in.at[1, pl.ds(0, 7 * 16)], gv_recv.at[1])
    for q in range(16):
        turn[1, pl.ds(q, 8, stride=16), :] = g_in[1, pl.ds(q * 8, 8)]
    lines[...] = turn[1, 0:L]

    for kind in range(3):
        for chunk in range(CHUNKS):
            if kind != INV:
                wait_bytes(s1.at[kind, pl.ds(0, 7 * 16 * PARTS[chunk][1])], mz_send.at[kind, chunk])
            wait_bytes(s2.at[kind, pl.ds(0, 7 * 16 * PARTS[chunk][1])], mg_send.at[kind, chunk])
    for at in range(4):
        wait_bytes(z_out.at[at, pl.ds(0, 7 * 16)], zv_send.at[at])
    for at in range(3):
        wait_bytes(g_out.at[at, pl.ds(0, 7 * 16)], gv_send.at[at])


def outputs(lines, corr, rem):
    final = lines[...].T
    corr[...] = final[0:W]
    rem[...] = final[W : 2 * W]


def on_device(rhs, coupling, fwd_coupling, bwd_coupling, block_inverse):
    f32 = jnp.float32
    vmem = pl.BlockSpec(memory_space=pltpu.VMEM)
    dma = pltpu.SemaphoreType.DMA
    mat = pltpu.VMEM((3, W * W, L), f32)
    small = pltpu.VMEM((W, L), f32)
    lines = pl.pallas_call(
        kernel,
        out_shape=jax.ShapeDtypeStruct((L, L), f32),
        in_specs=[pl.BlockSpec(memory_space=pl.ANY)] * 5,
        out_specs=vmem,
        scratch_shapes=[
            small, small, pltpu.VMEM((3, W * W, L), jnp.bfloat16), dma((5,)),
            pltpu.VMEM((2, W * W, L), f32), pltpu.VMEM((2, W * W + ROWS, L), f32), mat, mat,
            pltpu.VMEM((2, 6, W * W, L), f32), pltpu.VMEM((W * W + 8, L), f32), pltpu.VMEM((W * W, L), f32),
            pltpu.VMEM((W * W // 2, L), f32), pltpu.VMEM((W * W, L), f32),
            pltpu.VMEM((W + 8, L), f32), pltpu.VMEM((L, L), f32), pltpu.VMEM((2, L + 16, L), f32),
            pltpu.VMEM((4, L, L), f32), pltpu.VMEM((4, L + 16, L), f32),
            pltpu.VMEM((3, L, L), f32), pltpu.VMEM((3, L, L), f32),
            pltpu.VMEM((2, W, L), f32), pltpu.VMEM((2, 2, W, L), f32),
            small, small, small, small, small,
            dma((2, CHUNKS)), dma((2, CHUNKS)), dma((3, CHUNKS)), dma((3, CHUNKS)),
            dma((4,)), dma((4,)), dma((3,)), dma((3,)), dma((2, 2)), dma((2, 2)),
        ],
        compiler_params=pltpu.CompilerParams(
            collective_id=0, has_side_effects=True, vmem_limit_bytes=62 << 20
        ),
        name="both_applies",
    )(
        rhs.reshape(W, L), coupling.reshape(W, L), fwd_coupling.reshape(W * W, L),
        bwd_coupling.reshape(W * W, L), block_inverse.reshape(W * W, L),
    )
    corr, rem = pl.pallas_call(
        outputs,
        out_shape=(jax.ShapeDtypeStruct((W, L), f32),) * 2,
        in_specs=[vmem],
        out_specs=(vmem, vmem),
        name="outputs",
    )(lines)
    return corr.reshape(rhs.shape), rem.reshape(rhs.shape)


def solution(mesh):
    vector = P("azim", None, "axial", None)
    matrix = P("azim", None, None, "axial", None)
    return jax.shard_map(
        on_device,
        mesh=mesh,
        in_specs=(vector, vector, matrix, matrix, matrix),
        out_specs=(vector, vector),
        check_vma=False,
    )
```

```python
import functools

import jax
import jax.numpy as jnp
from jax import lax
from jax.experimental import pallas as pl
from jax.experimental.pallas import tpu as pltpu
from jax.sharding import PartitionSpec as P

MESH = pl.DeviceIdType.MESH
W = 48
L = 128
RUN = 8
PIECES = W * W // L
ROWS = PIECES * 16
PARTS = ((0, 9), (9, 6), (15, 3))
CHUNKS = len(PARTS)
FWD, BWD, INV = 0, 1, 2


def aligned(start, size):
    return pl.ds(start if isinstance(start, int) else pl.multiple_of(start, 8), size)


def part_rows(base, chunk):
    first, count = PARTS[chunk]
    return aligned(base + first * 16, count * 16)


def wait_bytes(ref, sem):
    pltpu.make_async_copy(ref, ref, sem).wait()


def matvec(load, vec_ref):
    acc = jnp.zeros((6, 8, L), jnp.float32)
    for a in range(W):
        acc = acc + load(a).reshape(6, 8, L) * vec_ref[pl.ds(a, 8, stride=0), :][None]
    return acc.reshape(W, L)


def kernel(
    rhs_in, coup_in, fwd_in, bwd_in, inv_in, lines, rhs, coup, blocks, in_sem,
    s1, r1, s2, r2, maps, early, dup, packed, inv_t,
    vec, stage, turn, z_out, z_in, g_out, g_in, halo_out, halo_in,
    c_t, rhs_t, coup_t, first, middle,
    mz_send, mz_recv, mg_send, mg_recv, zv_send, zv_recv, gv_send, gv_recv, h_send, h_recv,
):
    me = lax.axis_index("azim")
    station = lax.axis_index("axial")
    z = lax.rem(me, RUN)
    g = me // RUN
    loads = [
        pltpu.make_async_copy(src, dst, in_sem.at[at])
        for at, (src, dst) in enumerate((
            (fwd_in, blocks.at[FWD]), (rhs_in, rhs), (coup_in, coup), (inv_in, blocks.at[INV]), (bwd_in, blocks.at[BWD]),
        ))
    ]
    for load in loads:
        load.start()

    def z_peer(i):
        return {"azim": g * RUN + lax.rem(z + i, RUN)}

    def g_peer(i):
        return {"azim": lax.rem(g + i, RUN) * RUN + z}

    up = {"axial": lax.rem(station + 1, 4)}
    down = {"axial": lax.rem(station + 3, 4)}

    lane = lax.broadcasted_iota(jnp.int32, (W, L), 1)
    lane_z = lax.rem(lane, RUN)
    lane_g = lane // 16

    barrier = pltpu.get_barrier_semaphore()

    def greet(i, _):
        pl.semaphore_signal(barrier, inc=1, device_id=z_peer(i), device_id_type=MESH)
        pl.semaphore_signal(barrier, inc=1, device_id=g_peer(i), device_id_type=MESH)
        return 0

    lax.fori_loop(1, RUN, greet, 0)
    pl.semaphore_signal(barrier, inc=1, device_id=up, device_id_type=MESH)
    pl.semaphore_signal(barrier, inc=1, device_id=down, device_id_type=MESH)

    def remote(src, dst, send, recv, device):
        pltpu.make_async_remote_copy(
            src_ref=src, dst_ref=dst, send_sem=send, recv_sem=recv,
            device_id=device, device_id_type=MESH,
        ).start()

    def pack(kind, chunk):
        def body(step, _):
            for inner in range(3):
                t = step * 3 + inner
                piece = blocks[kind, pl.ds(pl.multiple_of(t * L, L), L), :].astype(jnp.float32).T
                for zo in range(RUN):
                    s1[kind, aligned(zo * ROWS + t * 16, 16)] = piece[zo * 16 : zo * 16 + 16]
            return 0

        lax.fori_loop(PARTS[chunk][0] // 3, sum(PARTS[chunk]) // 3, body, 0)

    def send_z(kind, chunk):
        for i in range(1, RUN):
            to = lax.rem(z + i, RUN)
            remote(
                s1.at[kind, part_rows(to * ROWS, chunk)],
                r1.at[kind, part_rows(z * ROWS, chunk)],
                mz_send.at[kind, chunk], mz_recv.at[kind, chunk], z_peer(i),
            )
        own = part_rows(z * ROWS, chunk)
        r1[kind, own] = s1[kind, own]

    def forward_g(kind, chunk):
        wait_bytes(r1.at[kind, pl.ds(0, 7 * 16 * PARTS[chunk][1])], mz_recv.at[kind, chunk])

        def body(t, _):
            for q in range(16):
                s2[kind, aligned((q // 2) * ROWS + t * 16 + (q % 2) * 8, 8)] = r1[
                    kind, pl.ds(t * 16 + q, 8, stride=ROWS), :
                ]
            return 0

        lax.fori_loop(PARTS[chunk][0], sum(PARTS[chunk]), body, 0)
        send_g(kind, chunk)

    def pack_g(kind, chunk):
        def body(t, _):
            turn[0, 0:L] = blocks[kind, pl.ds(pl.multiple_of(t * L, L), L), :].astype(jnp.float32).T
            for q in range(16):
                s2[kind, aligned((q // 2) * ROWS + t * 16 + (q % 2) * 8, 8)] = turn[0, pl.ds(q, 8, stride=16), :]
            return 0

        lax.fori_loop(PARTS[chunk][0], sum(PARTS[chunk]), body, 0)
        send_g(kind, chunk)

    def send_g(kind, chunk):
        for i in range(1, RUN):
            to = lax.rem(g + i, RUN)
            remote(
                s2.at[kind, part_rows(to * ROWS, chunk)],
                r2.at[kind, part_rows(g * ROWS, chunk)],
                mg_send.at[kind, chunk], mg_recv.at[kind, chunk], g_peer(i),
            )
        own = part_rows(g * ROWS, chunk)
        r2[kind, own] = s2[kind, own]

    def unpack(kind, chunk):
        wait_bytes(r2.at[kind, pl.ds(0, 7 * 16 * PARTS[chunk][1])], mg_recv.at[kind, chunk])

        def body(step, _):
            for inner in range(3):
                t = step * 3 + inner
                rows = [r2[kind, aligned(run * ROWS + t * 16, 16)] for run in range(RUN)]
                piece = jnp.concatenate(rows, axis=0).T
                if kind == INV:
                    inv_t[pl.ds(pl.multiple_of(t * L, L), L), :] = piece
                else:
                    maps[kind, 0, pl.ds(pl.multiple_of(t * L, L), L), :] = -piece
            return 0

        lax.fori_loop(PARTS[chunk][0] // 3, sum(PARTS[chunk]) // 3, body, 0)

    def earlier(value, distance, kind):
        return pltpu.roll(value, distance if kind == FWD else L - distance, 1)

    def inside(distance, kind):
        if distance >= 16:
            return lane_g >= distance // 16
        return lane_z >= distance if kind == FWD else lane_z < RUN - distance

    def compose(kind, level):
        distance = 1 << level if level < 3 else 16 << (level - 3)
        exists = inside(distance, kind)
        sub = lax.broadcasted_iota(jnp.int32, (W, L), 0)

        def shift(step, _):
            for inner in range(8):
                a = step * 8 + inner
                moved = earlier(maps[kind, level, aligned(a * W, W)], distance, kind)
                early[aligned(a * W, W)] = jnp.where(exists, moved, jnp.where(sub == a, 1.0, 0.0))
            return 0

        lax.fori_loop(0, W // 8, shift, 0)

        def product(four, _):
            acc = [jnp.zeros((6, 8, L), jnp.float32)] * 4
            for c in range(W):
                later = maps[kind, level, pl.ds(c * W, W)].reshape(6, 8, L)
                for i in range(4):
                    factor = early[pl.ds((four * 4 + i) * W + c, 8, stride=0), :]
                    acc[i] = acc[i] + later * factor[None]
            for i in range(4):
                maps[kind, level + 1, aligned((four * 4 + i) * W, W)] = acc[i].reshape(W, L)
            return 0

        lax.fori_loop(0, W // 4, product, 0)

    def paired_sweep(value):
        def add(state, level, entering):
            vec[0:W] = entering
            return state + apply_map(FWD, level)

        def moved(state, distance):
            return jnp.where(inside(distance, FWD), pltpu.roll(state, distance, 1), 0.0)

        state = value
        for level in range(3):
            state = add(state, level, moved(state, 1 << level))
        two_runs = add(state, 3, moved(state, 16))
        four_runs = add(two_runs, 4, moved(two_runs, 32))
        turn_end = pltpu.roll(add(four_runs, 5, moved(four_runs, 64)), 16, 1)
        wrapped = turn_end
        for runs in (1, 2, 4):
            wrapped = jnp.where(lane_g < runs, wrapped, pltpu.roll(wrapped, 16 * runs, 1))
        low = add(four_runs, 5, wrapped)
        high = add(four_runs, 5, pltpu.roll(low, 64, 1))
        leaving = jnp.where(lane_g < 4, low, high)
        entering = jnp.where(lane_g == 0, turn_end, pltpu.roll(leaving, 16, 1))
        for distance in (1, 2, 4):
            entering = jnp.where(RUN - 1 - lane_z < distance, entering, pltpu.roll(entering, L - distance, 1))
        return add(state, 3, entering)

    even = lane_z % 2 == 0
    low2 = lane_z % 4 < 2
    low4 = lane_z < 4
    share = (0, 24, 12, 36)

    def back(value, distance):
        return pltpu.roll(value, L - distance, 1)

    def ahead(value, distance):
        return pltpu.roll(value, distance, 1)

    def rows_of(ref, a):
        return ref[aligned(a * W, W)]

    def each(start, stop, width, do):
        def body(step, _):
            for inner in range(width):
                do(step * width + inner)
            return 0

        lax.fori_loop(start // width, stop // width, body, 0)

    def packed_product(start, stop, width, over, more=False):
        def body(step, _):
            places = [aligned((step * width + i) * W, W) for i in range(width)]
            zero = jnp.zeros((6, 8, L), jnp.float32)
            acc = [packed[place].reshape(6, 8, L) if more else zero for place in places]
            for c in over:
                later = dup[pl.ds(c * W, W)].reshape(6, 8, L)
                for i in range(width):
                    factor = early[pl.ds((step * width + i) * W + c, 8, stride=0), :]
                    acc[i] = acc[i] + later * factor[None]
            for i in range(width):
                packed[places[i]] = acc[i].reshape(W, L)
            return 0

        lax.fori_loop(start // width, stop // width, body, 0)

    one, two, four, eight = (maps.at[BWD, level] for level in range(4))

    def early_pair(a):
        early[aligned(a * W, W)] = jnp.where(even, back(rows_of(one, a), 1), rows_of(one, a + 24))

    def later_pair(c):
        value = rows_of(one, c)
        dup[aligned(c * W, W)] = jnp.where(even, value, ahead(value, 1))

    def tree_start():
        each(0, 16, 8, early_pair)
        each(0, 40, 8, later_pair)
        packed_product(0, 16, 4, range(40))

    def tree_rest():
        each(16, 24, 8, early_pair)
        each(40, 48, 8, later_pair)
        packed_product(0, 16, 4, range(40, 48), True)
        packed_product(16, 24, 4, range(48))

        def early_quad(a):
            early[aligned(a * W, W)] = jnp.where(low2, back(rows_of(packed, a), 2), rows_of(packed, a + 12))

        def full_pair(a):
            value = rows_of(packed, a)
            for at, full in ((a, jnp.where(even, value, ahead(value, 1))), (a + 24, jnp.where(even, back(value, 1), value))):
                two[aligned(at * W, W)] = full
                dup[aligned(at * W, W)] = jnp.where(low2, full, ahead(full, 2))

        each(0, 12, 6, early_quad)
        each(0, 24, 4, full_pair)
        packed_product(0, 12, 4, range(48))

        def early_eight(a):
            early[aligned(a * W, W)] = jnp.where(low4, back(rows_of(packed, a), 4), rows_of(packed, a + 6))

        def full_quad(a):
            value = rows_of(packed, a)
            evens = jnp.where(even, value, ahead(value, 1))
            odds = jnp.where(even, back(value, 1), value)
            for q, pair in enumerate((evens, odds, evens, odds)):
                full = jnp.where(low2, pair, ahead(pair, 2)) if q < 2 else jnp.where(low2, back(pair, 2), pair)
                four[aligned((a + share[q]) * W, W)] = full
                dup[aligned((a + share[q]) * W, W)] = jnp.where(low4, full, ahead(full, 4))

        each(0, 6, 6, early_eight)
        each(0, 12, 2, full_quad)
        packed_product(0, 6, 3, range(48))

        def full_eight(a):
            value = rows_of(packed, a)
            for zz in range(RUN):
                full = back(value, zz) if zz else value
                at = a + share[zz % 4] + (6 if zz >= 4 else 0)
                eight[aligned(at * W, W)] = jnp.where(lane_z == 4, rows_of(four, at), full)

        each(0, 6, 2, full_eight)

    def tree_sweep(value):
        def add(state, level, entering):
            vec[0:W] = entering
            return state + apply_map(BWD, level)

        state = add(value, 0, jnp.where(even, back(value, 1), 0.0))
        state = add(state, 1, jnp.where(lane_z % 4 == 0, back(state, 2), 0.0))
        state = add(state, 2, jnp.where(lane_z == 0, back(state, 4), 0.0))

        def run_step(n, carry):
            running, entering = carry
            moved = jnp.where(lane_z == 0, back(running, 16), 0.0)
            entering = jnp.where(RUN - 1 - lane_g == n - RUN, moved, entering)
            return add(state, 3, moved), entering

        running, entering = lax.fori_loop(1, 15, run_step, (state, jnp.zeros((W, L), jnp.float32)))
        entering = jnp.where(lane_g == 0, back(running, 16), entering)
        entering = jnp.where(lane_z == 0, entering, 0.0)
        at_four, at_six, at_seven = (ahead(entering, d) for d in (4, 6, 7))
        state = add(state, 3, entering + at_four)
        state = add(state, 1, jnp.where(lane_z == 2, back(state, 2), at_six))
        return add(state, 0, jnp.where(even, 0.0, jnp.where(lane_z == 7, at_seven, back(state, 1))))

    def apply_map(kind, level):
        return matvec(lambda a: maps[kind, level, pl.ds(a * W, W)], vec)

    def sweep(kind, value):
        state = value
        for level in range(3):
            distance = 1 << level
            moved = earlier(state, distance, kind)
            vec[0:W] = jnp.where(inside(distance, kind), moved, 0.0)
            state = state + apply_map(kind, level)
        order = lane_g if kind == FWD else RUN - 1 - lane_g

        def run_step(n, carry):
            running, entering = carry
            moved = earlier(running, 16, kind)
            entering = jnp.where(order == n - RUN, moved, entering)
            vec[0:W] = moved
            return state + apply_map(kind, 3), entering

        running, entering = lax.fori_loop(1, 15, run_step, (state, jnp.zeros((W, L), jnp.float32)))
        entering = jnp.where(order == RUN - 1, earlier(running, 16, kind), entering)
        place = RUN - 1 - lane_z if kind == FWD else lane_z
        for distance in (1, 2, 4):
            back = pltpu.roll(entering, L - distance if kind == FWD else distance, 1)
            entering = jnp.where(place < distance, entering, back)
        vec[0:W] = entering
        return state + apply_map(kind, 3)

    def g_stage(at, gather):
        for run in range(RUN):
            for half in range(2):
                g_out[at, run * 16 + half * 8 : run * 16 + half * 8 + 8] = gather(run, half)
        for i in range(1, RUN):
            to = lax.rem(g + i, RUN)
            remote(
                g_out.at[at, aligned(to * 16, 16)], g_in.at[at, aligned(g * 16, 16)],
                gv_send.at[at], gv_recv.at[at], g_peer(i),
            )
        g_in[at, aligned(g * 16, 16)] = g_out[at, aligned(g * 16, 16)]

    def z_start(at, value):
        stage[0:W] = value
        turn[0, 0:L] = stage[...].T
        for zz in range(RUN):
            for half in range(2):
                z_out[at, pl.ds(zz * 16 + half * 8, 8)] = turn[0, pl.ds(zz + 64 * half, 8, stride=8), :]
        for i in (4, 3, 5, 2, 6, 1, 7):
            to = lax.rem(z + i, RUN)
            remote(
                z_out.at[at, aligned(to * 16, 16)], z_in.at[at, aligned(z * 16, 16)],
                zv_send.at[at], zv_recv.at[at], z_peer(i),
            )
        z_in[at, aligned(z * 16, 16)] = z_out[at, aligned(z * 16, 16)]

    def z_finish(at):
        wait_bytes(z_in.at[at, pl.ds(0, 7 * 16)], zv_recv.at[at])
        for m in range(16):
            turn[0, m * 8 : m * 8 + 8] = z_in[at, pl.ds(m, 8, stride=16), :]
        return turn[0, 0:L].T[0:W]

    def stations_start(at, value):
        halo_out[at] = value
        remote(halo_out.at[at], halo_in.at[at, 0], h_send.at[at, 0], h_recv.at[at, 0], up)
        remote(halo_out.at[at], halo_in.at[at, 1], h_send.at[at, 1], h_recv.at[at, 1], down)

    def stations_finish(at):
        for side in range(2):
            wait_bytes(halo_in.at[at, side], h_recv.at[at, side])
            wait_bytes(halo_out.at[at], h_send.at[at, side])
        below = jnp.where(station > 0, halo_in[at, 0], 0.0)
        above = jnp.where(station < 3, halo_in[at, 1], 0.0)
        return below + above

    def inverse(ref):
        return matvec(lambda a: inv_t[pl.ds(a * W, W)], ref)

    loads[0].wait()
    for chunk in range(CHUNKS):
        pack(FWD, chunk)
        if chunk == 0:
            pl.semaphore_wait(barrier, 16)
        send_z(FWD, chunk)
    for load in loads[1:]:
        load.wait()
    vec[0:W] = rhs[...]
    stage[...] = jnp.zeros((L, L), jnp.float32)
    stage[0:W] = matvec(lambda a: blocks[INV, pl.ds(a * W, W), :].astype(jnp.float32), vec)
    stage[W : 2 * W] = rhs[...]
    turn[0, 0:L] = stage[...].T
    g_stage(0, lambda run, half: turn[0, pl.ds(run * 2 + half, 8, stride=16), :])
    stage[0:W] = coup[...]
    turn[1, 0:L] = stage[...].T
    g_stage(2, lambda run, half: turn[1, pl.ds(run * 2 + half, 8, stride=16), :])
    for chunk in range(CHUNKS):
        pack(BWD, chunk)
    wait_bytes(g_in.at[0, pl.ds(0, 7 * 16)], gv_recv.at[0])
    turned = g_in[0].T
    rhs_t[...] = turned[W : 2 * W]
    z_start(0, turned[0:W])
    for chunk in range(CHUNKS):
        send_z(BWD, chunk)
    for chunk in range(CHUNKS):
        pack_g(INV, chunk)
    for chunk in range(CHUNKS):
        forward_g(FWD, chunk)
    for chunk in range(CHUNKS):
        unpack(FWD, chunk)
    compose(FWD, 0)
    compose(FWD, 1)
    forward_g(BWD, 0)
    compose(FWD, 2)
    c_t[...] = z_finish(0)
    c_t[...] = sweep(FWD, c_t[...])
    forward_g(BWD, 1)
    forward_g(BWD, 2)
    unpack(BWD, 0)
    unpack(BWD, 1)
    tree_start()
    unpack(BWD, 2)
    tree_rest()

    z_start(1, tree_sweep(c_t[...]))
    compose(FWD, 3)
    first[...] = z_finish(1)
    stations_start(0, first[...])
    wait_bytes(g_in.at[2, pl.ds(0, 7 * 16)], gv_recv.at[2])
    coup_t[...] = g_in[2].T[0:W]
    for chunk in range(CHUNKS):
        unpack(INV, chunk)
    vec[0:W] = rhs_t[...] - first[...] + coup_t[...] * stations_finish(0)
    middle[...] = vec[0:W]
    z_start(2, inverse(vec))
    compose(FWD, 4)
    c_t[...] = z_finish(2)
    c_t[...] = paired_sweep(c_t[...])
    z_start(3, tree_sweep(c_t[...]))
    c_t[...] = z_finish(3)
    stations_start(1, c_t[...])
    stage[0:W] = first[...] + c_t[...]
    stage[W : 2 * W] = middle[...] - c_t[...] + coup_t[...] * stations_finish(1)
    turn[0, 0:L] = stage[...].T
    g_stage(1, lambda run, half: turn[0, pl.ds(run * 16 + half * 8, 8)])
    wait_bytes(g_in.at[1, pl.ds(0, 7 * 16)], gv_recv.at[1])
    for q in range(16):
        turn[1, pl.ds(q, 8, stride=16), :] = g_in[1, pl.ds(q * 8, 8)]
    lines[...] = turn[1, 0:L]

    for kind in range(3):
        for chunk in range(CHUNKS):
            if kind != INV:
                wait_bytes(s1.at[kind, pl.ds(0, 7 * 16 * PARTS[chunk][1])], mz_send.at[kind, chunk])
            wait_bytes(s2.at[kind, pl.ds(0, 7 * 16 * PARTS[chunk][1])], mg_send.at[kind, chunk])
    for at in range(4):
        wait_bytes(z_out.at[at, pl.ds(0, 7 * 16)], zv_send.at[at])
    for at in range(3):
        wait_bytes(g_out.at[at, pl.ds(0, 7 * 16)], gv_send.at[at])


def outputs(lines, corr, rem):
    final = lines[...].T
    corr[...] = final[0:W]
    rem[...] = final[W : 2 * W]


def on_device(rhs, coupling, fwd_coupling, bwd_coupling, block_inverse):
    f32 = jnp.float32
    vmem = pl.BlockSpec(memory_space=pltpu.VMEM)
    dma = pltpu.SemaphoreType.DMA
    mat = pltpu.VMEM((3, W * W, L), f32)
    small = pltpu.VMEM((W, L), f32)
    lines = pl.pallas_call(
        kernel,
        out_shape=jax.ShapeDtypeStruct((L, L), f32),
        in_specs=[pl.BlockSpec(memory_space=pl.ANY)] * 5,
        out_specs=vmem,
        scratch_shapes=[
            small, small, pltpu.VMEM((3, W * W, L), jnp.bfloat16), dma((5,)),
            pltpu.VMEM((2, W * W, L), f32), pltpu.VMEM((2, W * W + ROWS, L), f32), mat, mat,
            pltpu.VMEM((2, 6, W * W, L), f32), pltpu.VMEM((W * W + 8, L), f32), pltpu.VMEM((W * W, L), f32),
            pltpu.VMEM((W * W // 2, L), f32), pltpu.VMEM((W * W, L), f32),
            pltpu.VMEM((W + 8, L), f32), pltpu.VMEM((L, L), f32), pltpu.VMEM((2, L + 16, L), f32),
            pltpu.VMEM((4, L, L), f32), pltpu.VMEM((4, L + 16, L), f32),
            pltpu.VMEM((3, L, L), f32), pltpu.VMEM((3, L, L), f32),
            pltpu.VMEM((2, W, L), f32), pltpu.VMEM((2, 2, W, L), f32),
            small, small, small, small, small,
            dma((2, CHUNKS)), dma((2, CHUNKS)), dma((3, CHUNKS)), dma((3, CHUNKS)),
            dma((4,)), dma((4,)), dma((3,)), dma((3,)), dma((2, 2)), dma((2, 2)),
        ],
        compiler_params=pltpu.CompilerParams(
            collective_id=0, has_side_effects=True, vmem_limit_bytes=62 << 20
        ),
        name="both_applies",
    )(
        rhs.reshape(W, L), coupling.reshape(W, L), fwd_coupling.reshape(W * W, L),
        bwd_coupling.reshape(W * W, L), block_inverse.reshape(W * W, L),
    )
    corr, rem = pl.pallas_call(
        outputs,
        out_shape=(jax.ShapeDtypeStruct((W, L), f32),) * 2,
        in_specs=[vmem],
        out_specs=(vmem, vmem),
        name="outputs",
    )(lines)
    return corr.reshape(rhs.shape), rem.reshape(rhs.shape)


def solution(mesh):
    vector = P("azim", None, "axial", None)
    matrix = P("azim", None, None, "axial", None)
    return jax.shard_map(
        on_device,
        mesh=mesh,
        in_specs=(vector, vector, matrix, matrix, matrix),
        out_specs=(vector, vector),
        check_vma=False,
    )
```

```python
import functools

import jax
import jax.numpy as jnp
from jax import lax
from jax.experimental import pallas as pl
from jax.experimental.pallas import tpu as pltpu
from jax.sharding import PartitionSpec as P

MESH = pl.DeviceIdType.MESH
W = 48
L = 128
RUN = 8
PIECES = W * W // L
ROWS = PIECES * 16
PARTS = ((0, 9), (9, 6), (15, 3))
CHUNKS = len(PARTS)
FWD, BWD, INV = 0, 1, 2


def aligned(start, size):
    return pl.ds(start if isinstance(start, int) else pl.multiple_of(start, 8), size)


def part_rows(base, chunk):
    first, count = PARTS[chunk]
    return aligned(base + first * 16, count * 16)


def wait_bytes(ref, sem):
    pltpu.make_async_copy(ref, ref, sem).wait()


def matvec(load, vec_ref):
    acc = jnp.zeros((6, 8, L), jnp.float32)
    for a in range(W):
        acc = acc + load(a).reshape(6, 8, L) * vec_ref[pl.ds(a, 8, stride=0), :][None]
    return acc.reshape(W, L)


def kernel(
    rhs_in, coup_in, fwd_in, bwd_in, inv_in, lines, rhs, coup, blocks, in_sem,
    s1, r1, s2, r2, maps, early, dup, packed, inv_t,
    vec, stage, turn, z_out, z_in, g_out, g_in, halo_out, halo_in,
    c_t, rhs_t, coup_t, first, middle,
    mz_send, mz_recv, mg_send, mg_recv, zv_send, zv_recv, gv_send, gv_recv, h_send, h_recv,
):
    me = lax.axis_index("azim")
    station = lax.axis_index("axial")
    z = lax.rem(me, RUN)
    g = me // RUN
    loads = [
        pltpu.make_async_copy(src, dst, in_sem.at[at])
        for at, (src, dst) in enumerate((
            (fwd_in, blocks.at[FWD]), (rhs_in, rhs), (coup_in, coup), (inv_in, blocks.at[INV]), (bwd_in, blocks.at[BWD]),
        ))
    ]
    for load in loads:
        load.start()

    def z_peer(i):
        return {"azim": g * RUN + lax.rem(z + i, RUN)}

    def g_peer(i):
        return {"azim": lax.rem(g + i, RUN) * RUN + z}

    up = {"axial": lax.rem(station + 1, 4)}
    down = {"axial": lax.rem(station + 3, 4)}

    lane = lax.broadcasted_iota(jnp.int32, (W, L), 1)
    lane_z = lax.rem(lane, RUN)
    lane_g = lane // 16

    barrier = pltpu.get_barrier_semaphore()

    def greet(i, _):
        pl.semaphore_signal(barrier, inc=1, device_id=z_peer(i), device_id_type=MESH)
        pl.semaphore_signal(barrier, inc=1, device_id=g_peer(i), device_id_type=MESH)
        return 0

    lax.fori_loop(1, RUN, greet, 0)
    pl.semaphore_signal(barrier, inc=1, device_id=up, device_id_type=MESH)
    pl.semaphore_signal(barrier, inc=1, device_id=down, device_id_type=MESH)

    def remote(src, dst, send, recv, device):
        pltpu.make_async_remote_copy(
            src_ref=src, dst_ref=dst, send_sem=send, recv_sem=recv,
            device_id=device, device_id_type=MESH,
        ).start()

    def pack(kind, chunk):
        def body(step, _):
            for inner in range(3):
                t = step * 3 + inner
                piece = blocks[kind, pl.ds(pl.multiple_of(t * L, L), L), :].astype(jnp.float32).T
                for zo in range(RUN):
                    s1[kind, aligned(zo * ROWS + t * 16, 16)] = piece[zo * 16 : zo * 16 + 16]
            return 0

        lax.fori_loop(PARTS[chunk][0] // 3, sum(PARTS[chunk]) // 3, body, 0)

    def send_z(kind, chunk):
        for i in range(1, RUN):
            to = lax.rem(z + i, RUN)
            remote(
                s1.at[kind, part_rows(to * ROWS, chunk)],
                r1.at[kind, part_rows(z * ROWS, chunk)],
                mz_send.at[kind, chunk], mz_recv.at[kind, chunk], z_peer(i),
            )
        own = part_rows(z * ROWS, chunk)
        r1[kind, own] = s1[kind, own]

    def forward_g(kind, chunk):
        wait_bytes(r1.at[kind, pl.ds(0, 7 * 16 * PARTS[chunk][1])], mz_recv.at[kind, chunk])

        def body(t, _):
            for q in range(16):
                s2[kind, aligned((q // 2) * ROWS + t * 16 + (q % 2) * 8, 8)] = r1[
                    kind, pl.ds(t * 16 + q, 8, stride=ROWS), :
                ]
            return 0

        lax.fori_loop(PARTS[chunk][0], sum(PARTS[chunk]), body, 0)
        send_g(kind, chunk)

    def pack_g(kind, chunk):
        def body(t, _):
            turn[0, 0:L] = blocks[kind, pl.ds(pl.multiple_of(t * L, L), L), :].astype(jnp.float32).T
            for q in range(16):
                s2[kind, aligned((q // 2) * ROWS + t * 16 + (q % 2) * 8, 8)] = turn[0, pl.ds(q, 8, stride=16), :]
            return 0

        lax.fori_loop(PARTS[chunk][0], sum(PARTS[chunk]), body, 0)
        send_g(kind, chunk)

    def send_g(kind, chunk):
        for i in range(1, RUN):
            to = lax.rem(g + i, RUN)
            remote(
                s2.at[kind, part_rows(to * ROWS, chunk)],
                r2.at[kind, part_rows(g * ROWS, chunk)],
                mg_send.at[kind, chunk], mg_recv.at[kind, chunk], g_peer(i),
            )
        own = part_rows(g * ROWS, chunk)
        r2[kind, own] = s2[kind, own]

    def unpack(kind, chunk):
        wait_bytes(r2.at[kind, pl.ds(0, 7 * 16 * PARTS[chunk][1])], mg_recv.at[kind, chunk])

        def body(step, _):
            for inner in range(3):
                t = step * 3 + inner
                rows = [r2[kind, aligned(run * ROWS + t * 16, 16)] for run in range(RUN)]
                piece = jnp.concatenate(rows, axis=0).T
                if kind == INV:
                    inv_t[pl.ds(pl.multiple_of(t * L, L), L), :] = piece
                else:
                    maps[kind, 0, pl.ds(pl.multiple_of(t * L, L), L), :] = -piece
            return 0

        lax.fori_loop(PARTS[chunk][0] // 3, sum(PARTS[chunk]) // 3, body, 0)

    def earlier(value, distance, kind):
        return pltpu.roll(value, distance if kind == FWD else L - distance, 1)

    def inside(distance, kind):
        if distance >= 16:
            return lane_g >= distance // 16
        return lane_z >= distance if kind == FWD else lane_z < RUN - distance

    def compose(kind, level):
        distance = 1 << level if level < 3 else 16 << (level - 3)
        exists = inside(distance, kind)
        sub = lax.broadcasted_iota(jnp.int32, (W, L), 0)

        def shift(step, _):
            for inner in range(8):
                a = step * 8 + inner
                moved = earlier(maps[kind, level, aligned(a * W, W)], distance, kind)
                early[aligned(a * W, W)] = jnp.where(exists, moved, jnp.where(sub == a, 1.0, 0.0))
            return 0

        lax.fori_loop(0, W // 8, shift, 0)

        def product(four, _):
            acc = [jnp.zeros((6, 8, L), jnp.float32)] * 4
            for c in range(W):
                later = maps[kind, level, pl.ds(c * W, W)].reshape(6, 8, L)
                for i in range(4):
                    factor = early[pl.ds((four * 4 + i) * W + c, 8, stride=0), :]
                    acc[i] = acc[i] + later * factor[None]
            for i in range(4):
                maps[kind, level + 1, aligned((four * 4 + i) * W, W)] = acc[i].reshape(W, L)
            return 0

        lax.fori_loop(0, W // 4, product, 0)

    def paired_sweep(value):
        def add(state, level, entering):
            vec[0:W] = entering
            return state + apply_map(FWD, level)

        def moved(state, distance):
            return jnp.where(inside(distance, FWD), pltpu.roll(state, distance, 1), 0.0)

        state = value
        for level in range(3):
            state = add(state, level, moved(state, 1 << level))
        two_runs = add(state, 3, moved(state, 16))
        four_runs = add(two_runs, 4, moved(two_runs, 32))
        turn_end = pltpu.roll(add(four_runs, 5, moved(four_runs, 64)), 16, 1)
        wrapped = turn_end
        for runs in (1, 2, 4):
            wrapped = jnp.where(lane_g < runs, wrapped, pltpu.roll(wrapped, 16 * runs, 1))
        low = add(four_runs, 5, wrapped)
        high = add(four_runs, 5, pltpu.roll(low, 64, 1))
        leaving = jnp.where(lane_g < 4, low, high)
        entering = jnp.where(lane_g == 0, turn_end, pltpu.roll(leaving, 16, 1))
        for distance in (1, 2, 4):
            entering = jnp.where(RUN - 1 - lane_z < distance, entering, pltpu.roll(entering, L - distance, 1))
        return add(state, 3, entering)

    even = lane_z % 2 == 0
    low2 = lane_z % 4 < 2
    low4 = lane_z < 4
    share = (0, 24, 12, 36)

    def back(value, distance):
        return pltpu.roll(value, L - distance, 1)

    def ahead(value, distance):
        return pltpu.roll(value, distance, 1)

    def rows_of(ref, a):
        return ref[aligned(a * W, W)]

    def each(start, stop, width, do):
        def body(step, _):
            for inner in range(width):
                do(step * width + inner)
            return 0

        lax.fori_loop(start // width, stop // width, body, 0)

    def packed_product(start, stop, width, over, more=False):
        def body(step, _):
            places = [aligned((step * width + i) * W, W) for i in range(width)]
            zero = jnp.zeros((6, 8, L), jnp.float32)
            acc = [packed[place].reshape(6, 8, L) if more else zero for place in places]
            for c in over:
                later = dup[pl.ds(c * W, W)].reshape(6, 8, L)
                for i in range(width):
                    factor = early[pl.ds((step * width + i) * W + c, 8, stride=0), :]
                    acc[i] = acc[i] + later * factor[None]
            for i in range(width):
                packed[places[i]] = acc[i].reshape(W, L)
            return 0

        lax.fori_loop(start // width, stop // width, body, 0)

    one, two, four, eight = (maps.at[BWD, level] for level in range(4))

    def early_pair(a):
        early[aligned(a * W, W)] = jnp.where(even, back(rows_of(one, a), 1), rows_of(one, a + 24))

    def later_pair(c):
        value = rows_of(one, c)
        dup[aligned(c * W, W)] = jnp.where(even, value, ahead(value, 1))

    def tree_start():
        each(0, 16, 8, early_pair)
        each(0, 40, 8, later_pair)
        packed_product(0, 16, 4, range(40))

    def tree_rest():
        each(16, 24, 8, early_pair)
        each(40, 48, 8, later_pair)
        packed_product(0, 16, 4, range(40, 48), True)
        packed_product(16, 24, 4, range(48))

        def early_quad(a):
            early[aligned(a * W, W)] = jnp.where(low2, back(rows_of(packed, a), 2), rows_of(packed, a + 12))

        def full_pair(a):
            value = rows_of(packed, a)
            for at, full in ((a, jnp.where(even, value, ahead(value, 1))), (a + 24, jnp.where(even, back(value, 1), value))):
                two[aligned(at * W, W)] = full
                dup[aligned(at * W, W)] = jnp.where(low2, full, ahead(full, 2))

        each(0, 12, 6, early_quad)
        each(0, 24, 4, full_pair)
        packed_product(0, 12, 4, range(48))

        def early_eight(a):
            early[aligned(a * W, W)] = jnp.where(low4, back(rows_of(packed, a), 4), rows_of(packed, a + 6))

        def full_quad(a):
            value = rows_of(packed, a)
            evens = jnp.where(even, value, ahead(value, 1))
            odds = jnp.where(even, back(value, 1), value)
            for q, pair in enumerate((evens, odds, evens, odds)):
                full = jnp.where(low2, pair, ahead(pair, 2)) if q < 2 else jnp.where(low2, back(pair, 2), pair)
                four[aligned((a + share[q]) * W, W)] = full
                dup[aligned((a + share[q]) * W, W)] = jnp.where(low4, full, ahead(full, 4))

        each(0, 6, 6, early_eight)
        each(0, 12, 2, full_quad)
        packed_product(0, 6, 3, range(48))

        def full_eight(a):
            value = rows_of(packed, a)
            for zz in range(RUN):
                full = back(value, zz) if zz else value
                at = a + share[zz % 4] + (6 if zz >= 4 else 0)
                eight[aligned(at * W, W)] = jnp.where(lane_z == 4, rows_of(four, at), full)

        each(0, 6, 2, full_eight)

    def tree_sweep(value):
        def add(state, level, entering):
            vec[0:W] = entering
            return state + apply_map(BWD, level)

        state = add(value, 0, jnp.where(even, back(value, 1), 0.0))
        state = add(state, 1, jnp.where(lane_z % 4 == 0, back(state, 2), 0.0))
        state = add(state, 2, jnp.where(lane_z == 0, back(state, 4), 0.0))

        def run_step(n, carry):
            running, entering = carry
            moved = jnp.where(lane_z == 0, back(running, 16), 0.0)
            entering = jnp.where(RUN - 1 - lane_g == n - RUN, moved, entering)
            return add(state, 3, moved), entering

        running, entering = lax.fori_loop(1, 15, run_step, (state, jnp.zeros((W, L), jnp.float32)))
        entering = jnp.where(lane_g == 0, back(running, 16), entering)
        entering = jnp.where(lane_z == 0, entering, 0.0)
        at_four, at_six, at_seven = (ahead(entering, d) for d in (4, 6, 7))
        state = add(state, 3, entering + at_four)
        state = add(state, 1, jnp.where(lane_z == 2, back(state, 2), at_six))
        return add(state, 0, jnp.where(even, 0.0, jnp.where(lane_z == 7, at_seven, back(state, 1))))

    def apply_map(kind, level):
        return matvec(lambda a: maps[kind, level, pl.ds(a * W, W)], vec)

    def sweep(kind, value):
        state = value
        for level in range(3):
            distance = 1 << level
            moved = earlier(state, distance, kind)
            vec[0:W] = jnp.where(inside(distance, kind), moved, 0.0)
            state = state + apply_map(kind, level)
        order = lane_g if kind == FWD else RUN - 1 - lane_g

        def run_step(n, carry):
            running, entering = carry
            moved = earlier(running, 16, kind)
            entering = jnp.where(order == n - RUN, moved, entering)
            vec[0:W] = moved
            return state + apply_map(kind, 3), entering

        running, entering = lax.fori_loop(1, 15, run_step, (state, jnp.zeros((W, L), jnp.float32)))
        entering = jnp.where(order == RUN - 1, earlier(running, 16, kind), entering)
        place = RUN - 1 - lane_z if kind == FWD else lane_z
        for distance in (1, 2, 4):
            back = pltpu.roll(entering, L - distance if kind == FWD else distance, 1)
            entering = jnp.where(place < distance, entering, back)
        vec[0:W] = entering
        return state + apply_map(kind, 3)

    def g_stage(at, gather):
        for run in range(RUN):
            for half in range(2):
                g_out[at, run * 16 + half * 8 : run * 16 + half * 8 + 8] = gather(run, half)
        for i in (5, 3, 7, 1, 4, 2, 6):
            to = lax.rem(g + i, RUN)
            remote(
                g_out.at[at, aligned(to * 16, 16)], g_in.at[at, aligned(g * 16, 16)],
                gv_send.at[at], gv_recv.at[at], g_peer(i),
            )
        g_in[at, aligned(g * 16, 16)] = g_out[at, aligned(g * 16, 16)]

    def z_start(at, value):
        stage[0:W] = value
        turn[0, 0:L] = stage[...].T
        for zz in range(RUN):
            for half in range(2):
                z_out[at, pl.ds(zz * 16 + half * 8, 8)] = turn[0, pl.ds(zz + 64 * half, 8, stride=8), :]
        for i in (4, 3, 5, 2, 6, 1, 7):
            to = lax.rem(z + i, RUN)
            remote(
                z_out.at[at, aligned(to * 16, 16)], z_in.at[at, aligned(z * 16, 16)],
                zv_send.at[at], zv_recv.at[at], z_peer(i),
            )
        z_in[at, aligned(z * 16, 16)] = z_out[at, aligned(z * 16, 16)]

    def z_finish(at):
        wait_bytes(z_in.at[at, pl.ds(0, 7 * 16)], zv_recv.at[at])
        for m in range(16):
            turn[0, m * 8 : m * 8 + 8] = z_in[at, pl.ds(m, 8, stride=16), :]
        return turn[0, 0:L].T[0:W]

    def stations_start(at, value):
        halo_out[at] = value
        remote(halo_out.at[at], halo_in.at[at, 0], h_send.at[at, 0], h_recv.at[at, 0], up)
        remote(halo_out.at[at], halo_in.at[at, 1], h_send.at[at, 1], h_recv.at[at, 1], down)

    def stations_finish(at):
        for side in range(2):
            wait_bytes(halo_in.at[at, side], h_recv.at[at, side])
        below = jnp.where(station > 0, halo_in[at, 0], 0.0)
        above = jnp.where(station < 3, halo_in[at, 1], 0.0)
        return below + above

    def inverse(ref):
        return matvec(lambda a: inv_t[pl.ds(a * W, W)], ref)

    loads[0].wait()
    for chunk in range(CHUNKS):
        pack(FWD, chunk)
        if chunk == 0:
            pl.semaphore_wait(barrier, 16)
        send_z(FWD, chunk)
    for load in loads[1:]:
        load.wait()
    vec[0:W] = rhs[...]
    stage[...] = jnp.zeros((L, L), jnp.float32)
    stage[0:W] = matvec(lambda a: blocks[INV, pl.ds(a * W, W), :].astype(jnp.float32), vec)
    stage[W : 2 * W] = rhs[...]
    turn[0, 0:L] = stage[...].T
    g_stage(0, lambda run, half: turn[0, pl.ds(run * 2 + half, 8, stride=16), :])
    stage[0:W] = coup[...]
    turn[1, 0:L] = stage[...].T
    g_stage(2, lambda run, half: turn[1, pl.ds(run * 2 + half, 8, stride=16), :])
    for chunk in range(CHUNKS):
        pack(BWD, chunk)
    wait_bytes(g_in.at[0, pl.ds(0, 7 * 16)], gv_recv.at[0])
    turned = g_in[0].T
    rhs_t[...] = turned[W : 2 * W]
    z_start(0, turned[0:W])
    for chunk in range(CHUNKS):
        send_z(BWD, chunk)
    for chunk in range(CHUNKS):
        pack_g(INV, chunk)
    for chunk in range(CHUNKS):
        forward_g(FWD, chunk)
    for chunk in range(CHUNKS):
        unpack(FWD, chunk)
    compose(FWD, 0)
    compose(FWD, 1)
    forward_g(BWD, 0)
    compose(FWD, 2)
    c_t[...] = z_finish(0)
    c_t[...] = sweep(FWD, c_t[...])
    forward_g(BWD, 1)
    forward_g(BWD, 2)
    unpack(BWD, 0)
    unpack(BWD, 1)
    tree_start()
    unpack(BWD, 2)
    tree_rest()

    z_start(1, tree_sweep(c_t[...]))
    compose(FWD, 3)
    first[...] = z_finish(1)
    stations_start(0, first[...])
    wait_bytes(g_in.at[2, pl.ds(0, 7 * 16)], gv_recv.at[2])
    coup_t[...] = g_in[2].T[0:W]
    for chunk in range(CHUNKS):
        unpack(INV, chunk)
    vec[0:W] = rhs_t[...] - first[...] + coup_t[...] * stations_finish(0)
    middle[...] = vec[0:W]
    z_start(2, inverse(vec))
    compose(FWD, 4)
    c_t[...] = z_finish(2)
    c_t[...] = paired_sweep(c_t[...])
    z_start(3, tree_sweep(c_t[...]))
    c_t[...] = z_finish(3)
    stations_start(1, c_t[...])
    stage[0:W] = first[...] + c_t[...]
    stage[W : 2 * W] = middle[...] - c_t[...] + coup_t[...] * stations_finish(1)
    turn[0, 0:L] = stage[...].T
    g_stage(1, lambda run, half: turn[0, pl.ds(run * 16 + half * 8, 8)])
    wait_bytes(g_in.at[1, pl.ds(0, 7 * 16)], gv_recv.at[1])
    for q in range(16):
        turn[1, pl.ds(q, 8, stride=16), :] = g_in[1, pl.ds(q * 8, 8)]
    lines[...] = turn[1, 0:L]

    for kind in range(3):
        for chunk in range(CHUNKS):
            if kind != INV:
                wait_bytes(s1.at[kind, pl.ds(0, 7 * 16 * PARTS[chunk][1])], mz_send.at[kind, chunk])
            wait_bytes(s2.at[kind, pl.ds(0, 7 * 16 * PARTS[chunk][1])], mg_send.at[kind, chunk])
    for at in range(2):
        for side in range(2):
            wait_bytes(halo_out.at[at], h_send.at[at, side])
    for at in range(4):
        wait_bytes(z_out.at[at, pl.ds(0, 7 * 16)], zv_send.at[at])
    for at in range(3):
        wait_bytes(g_out.at[at, pl.ds(0, 7 * 16)], gv_send.at[at])


def outputs(lines, corr, rem):
    final = lines[...].T
    corr[...] = final[0:W]
    rem[...] = final[W : 2 * W]


def on_device(rhs, coupling, fwd_coupling, bwd_coupling, block_inverse):
    f32 = jnp.float32
    vmem = pl.BlockSpec(memory_space=pltpu.VMEM)
    dma = pltpu.SemaphoreType.DMA
    mat = pltpu.VMEM((3, W * W, L), f32)
    small = pltpu.VMEM((W, L), f32)
    lines = pl.pallas_call(
        kernel,
        out_shape=jax.ShapeDtypeStruct((L, L), f32),
        in_specs=[pl.BlockSpec(memory_space=pl.ANY)] * 5,
        out_specs=vmem,
        scratch_shapes=[
            small, small, pltpu.VMEM((3, W * W, L), jnp.bfloat16), dma((5,)),
            pltpu.VMEM((2, W * W, L), f32), pltpu.VMEM((2, W * W + ROWS, L), f32), mat, mat,
            pltpu.VMEM((2, 6, W * W, L), f32), pltpu.VMEM((W * W + 8, L), f32), pltpu.VMEM((W * W, L), f32),
            pltpu.VMEM((W * W // 2, L), f32), pltpu.VMEM((W * W, L), f32),
            pltpu.VMEM((W + 8, L), f32), pltpu.VMEM((L, L), f32), pltpu.VMEM((2, L + 16, L), f32),
            pltpu.VMEM((4, L, L), f32), pltpu.VMEM((4, L + 16, L), f32),
            pltpu.VMEM((3, L, L), f32), pltpu.VMEM((3, L, L), f32),
            pltpu.VMEM((2, W, L), f32), pltpu.VMEM((2, 2, W, L), f32),
            small, small, small, small, small,
            dma((2, CHUNKS)), dma((2, CHUNKS)), dma((3, CHUNKS)), dma((3, CHUNKS)),
            dma((4,)), dma((4,)), dma((3,)), dma((3,)), dma((2, 2)), dma((2, 2)),
        ],
        compiler_params=pltpu.CompilerParams(
            collective_id=0, has_side_effects=True, vmem_limit_bytes=62 << 20
        ),
        name="both_applies",
    )(
        rhs.reshape(W, L), coupling.reshape(W, L), fwd_coupling.reshape(W * W, L),
        bwd_coupling.reshape(W * W, L), block_inverse.reshape(W * W, L),
    )
    corr, rem = pl.pallas_call(
        outputs,
        out_shape=(jax.ShapeDtypeStruct((W, L), f32),) * 2,
        in_specs=[vmem],
        out_specs=(vmem, vmem),
        name="outputs",
    )(lines)
    return corr.reshape(rhs.shape), rem.reshape(rhs.shape)


def solution(mesh):
    vector = P("azim", None, "axial", None)
    matrix = P("azim", None, None, "axial", None)
    return jax.shard_map(
        on_device,
        mesh=mesh,
        in_specs=(vector, vector, matrix, matrix, matrix),
        out_specs=(vector, vector),
        check_vma=False,
    )
```
